1024 devices in a mesh: ctx: 128 (over z, y), chan: 8 (over x, core).
Axes of the slice: x: 4, y: 4, z: 32, core: 2. Of those that a mesh axis runs over, the one named last changes fastest.
Arguments:
- query: bfloat16 [1, 16384, 8192], P(None, 'ctx', 'chan'), may hold values from -6 to 6
- key_in: bfloat16 [1, 16384, 8192], P(None, 'ctx', 'chan'), may hold values from -6 to 6
- value_in: bfloat16 [1, 16384, 8192], P(None, 'ctx', 'chan'), may hold values from -6 to 6
- cotangent: bfloat16 [1, 16384, 8192], P(None, 'ctx', 'chan'), may hold values from -6 to 6
- filters: float32 [512, 128], P('chan'), may hold values from -0.5 to 0.5
- norm_gain: float32 [8192], P('chan'), may hold values from 0.1 to 1.9
Outputs:
- normed: bfloat16 [1, 16384, 8192], P(None, 'ctx', 'chan')
- grad_query: bfloat16 [1, 16384, 8192], P(None, 'ctx', 'chan')
- grad_key: bfloat16 [1, 16384, 8192], P(None, 'ctx', 'chan')
- grad_value: bfloat16 [1, 16384, 8192], P(None, 'ctx', 'chan')
- grad_filters: float32 [512, 128], P('chan')
The draws below stay inside these ranges and needn't reach their ends.
All inputs are finite; a program needn't handle non-finite values.
Results may differ from the reference program's by a relative error of at most 0.0058.
Values may be sent and summed in bfloat16 or wider, within the bound.
No kernel may reach another device: no remote copies, remote signals or barrier semaphores. Data moves between devices by JAX's collectives and lax.ppermute only.
A program may use at most 64 MiB of HBM per device.

```python
import jax
import jax.numpy as jnp
from jax import lax

D = 8192
GROUPS = 512
TAPS = 128
BATCH = 1
LENGTH = 16384


def block_scale(key, dims, cuts, low, largest):
    level, own = 1.0, jax.random.fold_in(key, 6)
    for dim, parts in cuts:
        heights = jnp.exp(jax.random.uniform(jax.random.fold_in(own, dim), (parts,), jnp.float32, low / len(cuts), largest / len(cuts)))
        level = level * jnp.repeat(heights, dims[dim] // parts).reshape([-1 if axis == dim else 1 for axis in range(len(dims))])
    return level


def centred(key, dims, scale, most, split=(), kind=jnp.bfloat16):
    level = block_scale(key, dims, split, -0.22, 0.18) if split else 1.0
    result = jax.random.normal(key, dims, jnp.float32) * scale * level
    return jnp.minimum(jnp.maximum(result, -most), most).astype(kind)


def setup_inputs(seed: int = 0) -> dict:
    key_list = jax.random.split(jax.random.key(seed), 7)
    return {
        "query": centred(key_list[0], (BATCH, LENGTH, D), 1.0, 6.0, ((1, 128), (2, 8))),
        "key_in": centred(key_list[1], (BATCH, LENGTH, D), 1.0, 6.0, ((1, 128), (2, 8))),
        "value_in": centred(key_list[2], (BATCH, LENGTH, D), 1.0, 6.0, ((1, 128), (2, 8))),
        "cotangent": centred(key_list[3], (BATCH, LENGTH, D), 1.0, 6.0, ((1, 128), (2, 8))),
        "filters": centred(key_list[4], (GROUPS, TAPS), TAPS ** -0.5, 0.5, ((0, 8),), jnp.float32),
        "norm_gain": jnp.clip(1.0 + 0.18 * jax.random.normal(key_list[5], (D,), jnp.float32), 0.1, 1.9),
    }


def toeplitz(taps):
    count, width = taps.shape
    zeros = jnp.zeros((count, width), taps.dtype)
    line = jnp.concatenate([zeros, jnp.flip(taps, 1), zeros], axis=1)
    tiled = jnp.tile(line, (1, width))
    tiled = tiled[:, :width * (3 * width - 1)].reshape(count, width, 3 * width - 1)
    return tiled[:, :, width - 1:3 * width - 1]

def lag_sums(pairs):
    count, width, double = pairs.shape
    flat = pairs.reshape(count, width * double)
    flat = jnp.concatenate([flat, jnp.zeros((count, width), pairs.dtype)], axis=1)
    skewed = flat.reshape(count, width, double + 1)
    totals = lax.optimization_barrier(jnp.sum(skewed, axis=1))
    return jnp.flip(totals[:, 1:width + 1], axis=1)

def reference(query, key_in, value_in, cotangent, filters, norm_gain):
    batch, length, width = query.shape
    groups, taps = filters.shape
    per = width // groups
    blocks_n = length // taps
    slabs = 8
    slab_groups = groups // slabs
    slab_width = slab_groups * per
    weights_all = toeplitz(filters.astype(jnp.bfloat16)).astype(jnp.float32)
    signal = (key_in.astype(jnp.float32) * value_in.astype(jnp.float32)).astype(jnp.bfloat16)
    windows = []
    mixed_parts = []
    for slab in range(slabs):
        lo = slab * slab_width
        weights = weights_all[slab * slab_groups:(slab + 1) * slab_groups]
        blocks = signal[:, :, lo:lo + slab_width].reshape(batch, blocks_n, taps, slab_groups, per)
        before = jnp.concatenate([jnp.zeros_like(blocks[:, :1]), blocks[:, :-1]], axis=1)
        window = jnp.concatenate([before, blocks], axis=2).reshape(batch * blocks_n, 2 * taps, slab_groups, per)
        windows.append(window)
        part = jnp.einsum('gts,bsgc->btgc', weights, window.astype(jnp.float32), precision=lax.Precision.HIGHEST)
        mixed_parts.append(part.reshape(batch, length, slab_width))
    mixed = jnp.concatenate(mixed_parts, axis=2)
    lifted = query.astype(jnp.float32) * mixed
    scaled = norm_gain * cotangent.astype(jnp.float32)
    power = lax.optimization_barrier(jnp.sum(lifted * lifted, axis=-1))
    inner = lax.optimization_barrier(jnp.sum(scaled * lifted, axis=-1))[..., None]
    recip = lax.rsqrt(power / D + 1e-06)[..., None]
    normed = (lifted * recip * norm_gain).astype(jnp.bfloat16)
    grad_mix = recip * scaled - lifted * recip ** 3 * inner / D
    grad_query = (grad_mix * mixed).astype(jnp.bfloat16)
    grad_conv = (grad_mix * query.astype(jnp.float32)).astype(jnp.bfloat16)
    extended = jnp.concatenate([grad_conv, jnp.zeros((batch, taps, width), jnp.bfloat16)], axis=1)
    grad_parts = []
    filter_parts = []
    for slab in range(slabs):
        lo = slab * slab_width
        weights = weights_all[slab * slab_groups:(slab + 1) * slab_groups]
        gathered = extended[:, :, lo:lo + slab_width].reshape(batch * (blocks_n + 1), taps, slab_groups, per)
        back = jnp.einsum('gts,btgc->bsgc', weights, gathered.astype(jnp.float32), precision=lax.Precision.HIGHEST)
        back = back.reshape(batch, blocks_n + 1, 2 * taps, slab_width)
        grad_parts.append((back[:, :blocks_n, taps:] + back[:, 1:, :taps]).reshape(batch, length, slab_width))
        own = grad_conv[:, :, lo:lo + slab_width].reshape(batch * blocks_n, taps, slab_groups, per)
        pairs = jnp.einsum('btgc,bsgc->gts', own.astype(jnp.float32), windows[slab].astype(jnp.float32), precision=lax.Precision.HIGHEST)
        filter_parts.append(lag_sums(pairs))
    grad_signal = jnp.concatenate(grad_parts, axis=2)
    grad_key = (grad_signal * value_in.astype(jnp.float32)).astype(jnp.bfloat16)
    grad_value = (grad_signal * key_in.astype(jnp.float32)).astype(jnp.bfloat16)
    grad_filters = jnp.concatenate(filter_parts, axis=0)
    return (normed, grad_query, grad_key, grad_value, grad_filters)
```

```python
import functools

import jax
import jax.numpy as jnp
from jax import lax
from jax.experimental import pallas as pl
from jax.experimental.pallas import tpu as pltpu
from jax.sharding import Mesh
from jax.sharding import PartitionSpec as P

D = 8192
CTX = ("zh", "zl", "y")
NEAR = ("zl", "y")
FAR = "zh"
LANES = 128
F32 = jnp.float32
BF16 = jnp.bfloat16


def shifted(block, axes, distance):
    devices = range(lax.axis_size(axes))
    route = [(i - distance, i) for i in devices if i - distance in devices]
    return lax.ppermute(block, axes, route)


def exchanged(x, axes):
    return lax.all_to_all(x, axes, 0, 0, tiled=True)


def call(kernel, outs, *args, flops=0, scratch=()):
    moved = sum(a.size * a.dtype.itemsize for a in args)
    moved += sum(o.size * o.dtype.itemsize for o in outs)
    vmem = pl.BlockSpec(memory_space=pltpu.VMEM)
    return pl.pallas_call(
        kernel,
        out_shape=outs,
        in_specs=[vmem] * len(args),
        out_specs=[vmem] * len(outs),
        scratch_shapes=scratch,
        cost_estimate=pl.CostEstimate(flops=flops, bytes_accessed=moved, transcendentals=0),
    )(*args)


def shaped(shape, dtype):
    return jax.ShapeDtypeStruct(shape, dtype)


def rolled(row, taps, shift=0):
    full = jnp.broadcast_to(row, (taps, row.shape[1]))
    return pltpu.roll(full, shift, 1, stride=1, stride_axis=0)


def index(shape, dim):
    return lax.broadcasted_iota(jnp.int32, shape, dim)


def column(row, taps):
    return jnp.broadcast_to(row, (taps, taps)).T


def lane_total(x):
    parts = [x[:, i : i + LANES] for i in range(0, x.shape[1], LANES)]
    while len(parts) > 1:
        parts = [a + b for a, b in zip(parts[::2], parts[1::2])]
    return jnp.sum(parts[0].T, axis=0, keepdims=True)


def signal_kernel(key_ref, value_ref, signal_ref):
    signal_ref[...] = (key_ref[...].astype(F32) * value_ref[...].astype(F32)).astype(BF16)


def weights_kernel(back_taps_ref, signal_ref, weights_ref, mirror_ref):
    groups, taps = back_taps_ref.shape
    row, col = index((taps, taps), 0), index((taps, taps), 1)
    own = row >= col

    def step(g, _):
        c = rolled(back_taps_ref[pl.ds(g, 1), :], taps)
        weights_ref[g, :, :taps] = jnp.where(own, 0.0, c).astype(BF16)
        weights_ref[g, :, taps:] = jnp.where(own, c, 0.0).astype(BF16)
        return 0

    lax.fori_loop(0, groups, step, 0, unroll=4)
    swap = (row + col == taps - 1).astype(BF16)
    mirror_ref[...] = jnp.dot(swap, signal_ref[...], preferred_element_type=F32).astype(BF16)


def mix_kernel(weights_ref, before_ref, signal_ref, query_ref, cot_ref, gain_ref, mixed_ref, sums_ref):
    groups, taps, _ = weights_ref.shape
    width = signal_ref.shape[1]
    per_tile = groups * LANES // width
    members = LANES // per_tile
    owner = index((taps, LANES), 1) // members

    def step(i, totals):
        lanes = pl.ds(pl.multiple_of(i * LANES, LANES), LANES)
        window = jnp.concatenate([before_ref[:, lanes], signal_ref[:, lanes]], axis=0)
        acc = None
        for k in range(per_tile):
            out = jnp.dot(weights_ref[i * per_tile + k], window, preferred_element_type=F32)
            acc = out if acc is None else jnp.where(owner == k, out, acc)
        mixed_ref[:, lanes] = acc
        lifted = query_ref[:, lanes].astype(F32) * acc
        scaled = gain_ref[:, lanes] * cot_ref[:, lanes].astype(F32)
        return totals[0] + lifted * lifted, totals[1] + scaled * lifted

    zero = jnp.zeros((taps, LANES), F32)
    power, inner = lax.fori_loop(0, width // LANES, step, (zero, zero))
    sums = jnp.concatenate(
        [jnp.sum(power.T, axis=0, keepdims=True), jnp.sum(inner.T, axis=0, keepdims=True)], axis=0
    )
    sums_ref[...] = jnp.broadcast_to(sums[None], sums_ref.shape)


def norm_terms(sums_ref, taps):
    sums = jnp.sum(sums_ref[...], axis=0)
    recip = lax.rsqrt(sums[0:1] / D + 1e-6)
    pull = recip * recip * recip * sums[1:2] / D
    return column(recip, taps), column(pull, taps)


def grad_kernel(sums_ref, mixed_ref, query_ref, cot_ref, gain_ref, conv_ref):
    taps, width = mixed_ref.shape
    recip, pull = norm_terms(sums_ref, taps)
    for i in range(0, width, LANES):
        lanes = slice(i, i + LANES)
        query = query_ref[:, lanes].astype(F32)
        scaled = gain_ref[:, lanes] * cot_ref[:, lanes].astype(F32)
        grad_mix = recip * scaled - query * mixed_ref[:, lanes] * pull
        conv_ref[:, lanes] = (grad_mix * query).astype(BF16)


def filter_kernel(conv_ref, before_ref, mirror_ref, totals_ref):
    taps, width = conv_ref.shape
    pieces, per_piece, _ = totals_ref.shape
    groups = pieces * per_piece
    per_tile = groups * LANES // width
    members = LANES // per_tile
    row, col = index((taps, taps), 0), index((taps, taps), 1)
    own = row + col >= taps - 1
    swap = (row + col == taps - 1).astype(BF16)
    owner = col // members

    def step(i, _):
        lanes = pl.ds(pl.multiple_of(i * LANES, LANES), LANES)
        conv = conv_ref[:, lanes]
        past = jnp.dot(swap, before_ref[:, lanes], preferred_element_type=F32).astype(BF16)
        window = jnp.concatenate([past, mirror_ref[:, lanes]], axis=0)
        found = []
        for k in range(per_tile):
            mine = jnp.where(owner == k, conv, jnp.zeros_like(conv))
            pairs = lax.dot_general(
                mine, window, (((1,), (1,)), ((), ())), preferred_element_type=F32
            )
            both = jnp.where(own, pairs[:, taps:], pairs[:, :taps])
            lined = pltpu.roll(both, 1, 1, stride=1, stride_axis=0)
            found.append(jnp.sum(lined, axis=0, keepdims=True))
        for k in range(0, per_tile, per_piece):
            totals_ref[i * (per_tile // per_piece) + k // per_piece] = jnp.concatenate(
                found[k : k + per_piece], axis=0
            )
        return 0

    lax.fori_loop(0, width // LANES, step, 0)


def output_kernel(sums_ref, mixed_ref, query_ref, cot_ref, gain_ref, normed_ref, query_grad_ref):
    taps, width = mixed_ref.shape
    recip, pull = norm_terms(sums_ref, taps)
    for i in range(0, width, LANES):
        lanes = slice(i, i + LANES)
        mixed = mixed_ref[:, lanes]
        lifted = query_ref[:, lanes].astype(F32) * mixed
        scaled = gain_ref[:, lanes] * cot_ref[:, lanes].astype(F32)
        normed_ref[:, lanes] = (lifted * recip * gain_ref[:, lanes]).astype(BF16)
        query_grad_ref[:, lanes] = ((recip * scaled - lifted * pull) * mixed).astype(BF16)


def back_kernel(taps_ref, conv_ref, after_ref, key_ref, value_ref, key_grad_ref, value_grad_ref):
    groups, taps = taps_ref.shape
    width = conv_ref.shape[1]
    per_tile = groups * LANES // width
    members = LANES // per_tile
    row, col = index((taps, taps), 0), index((taps, taps), 1)
    own = col >= row
    owner = col // members

    def step(i, _):
        lanes = pl.ds(pl.multiple_of(i * LANES, LANES), LANES)
        window = jnp.concatenate([conv_ref[:, lanes], after_ref[:, lanes]], axis=0)
        acc = None
        for k in range(per_tile):
            c = rolled(taps_ref[pl.ds(i * per_tile + k, 1), :], taps)
            weights = jnp.concatenate(
                [jnp.where(own, c, 0.0).astype(BF16), jnp.where(own, 0.0, c).astype(BF16)], axis=1
            )
            out = jnp.dot(weights, window, preferred_element_type=F32)
            acc = out if acc is None else jnp.where(owner == k, out, acc)
        key_grad_ref[:, lanes] = (acc * value_ref[:, lanes].astype(F32)).astype(BF16)
        value_grad_ref[:, lanes] = (acc * key_ref[:, lanes].astype(F32)).astype(BF16)
        return 0

    lax.fori_loop(0, width // LANES, step, 0)


def gather_sum_kernel(parts_ref, out_ref):
    out_ref[...] = jnp.broadcast_to(jnp.sum(parts_ref[...], axis=0)[None], out_ref.shape)


def body(query, key_in, value_in, cotangent, filters, norm_gain):
    _, taps, width = query.shape
    groups = filters.shape[0]
    query, key_in, value_in, cotangent = (
        a.reshape(taps, width) for a in (query, key_in, value_in, cotangent)
    )
    gain = norm_gain.reshape(1, width)
    rounded = filters.astype(BF16).astype(F32)
    back_taps = jnp.roll(jnp.flip(rounded, 1), 1, axis=1)
    block = shaped((taps, width), BF16)
    peers = lax.axis_size("chan")
    near, far = lax.axis_size(NEAR), lax.axis_size(FAR)
    conv_flops = 4 * groups * taps * taps * LANES

    (signal,) = call(signal_kernel, [block], key_in, value_in)
    before = shifted(signal, CTX, 1)
    weights, mirror = call(
        weights_kernel, [shaped((groups, taps, 2 * taps), BF16), block], back_taps, signal
    )
    mixed, sums = call(
        mix_kernel,
        [shaped((taps, width), F32), shaped((peers, 2, taps), F32)],
        weights, before, signal, query, cotangent, gain,
        flops=conv_flops,
    )
    sums = exchanged(sums, "chan")
    (conv,) = call(grad_kernel, [block], sums, mixed, query, cotangent, gain)
    (totals,) = call(
        filter_kernel, [shaped((near, groups // near, taps), F32)], conv, before, mirror,
        flops=conv_flops,
    )
    totals = exchanged(totals, NEAR)
    after = shifted(conv, CTX, -1)
    normed, grad_query = call(
        output_kernel, [block, block], sums, mixed, query, cotangent, gain
    )
    (totals,) = call(
        gather_sum_kernel, [shaped((far, groups // near, taps), F32)], totals
    )
    totals = exchanged(totals, FAR)
    grad_key, grad_value = call(
        back_kernel, [block, block], rounded, conv, after, key_in, value_in, flops=conv_flops
    )
    (totals,) = call(
        gather_sum_kernel, [shaped((near, groups // near, taps), F32)], totals
    )
    grad_filters = exchanged(totals, NEAR).reshape(groups, taps)
    return tuple(a[None] for a in (normed, grad_query, grad_key, grad_value)) + (grad_filters,)


def solution(mesh):
    torus = Mesh(
        mesh.devices.reshape(8, 4, 4, mesh.shape["chan"]), ("zh", "zl", "y", "chan")
    )
    rows = P(None, CTX, "chan")
    in_specs = (rows, rows, rows, rows, P("chan", None), P("chan"))
    out_specs = (rows, rows, rows, rows, P("chan", None))
    return jax.shard_map(body, mesh=torus, in_specs=in_specs, out_specs=out_specs, check_vma=False)
```

```python
import jax
import jax.numpy as jnp
from jax import lax
from jax.experimental import pallas as pl
from jax.experimental.pallas import tpu as pltpu
from jax.sharding import Mesh
from jax.sharding import PartitionSpec as P


D = 8192
CTX = ("zh", "zl", "y")
NEAR = ("zl", "y")
FAR = "zh"
LANES = 128
VMEM_LIMIT = 16 * 2**20
F32 = jnp.float32
BF16 = jnp.bfloat16


def shifted(block, axes, distance):
    devices = range(lax.axis_size(axes))
    route = [(i - distance, i) for i in devices if i - distance in devices]
    return lax.ppermute(block, axes, route)


def exchanged(x, axes, groups=None):
    return lax.all_to_all(x, axes, 0, 0, axis_index_groups=groups, tiled=True)


def call(kernel, outs, *args, flops=0, scratch=()):
    moved = sum(a.size * a.dtype.itemsize for a in args)
    moved += sum(o.size * o.dtype.itemsize for o in outs)
    vmem = pl.BlockSpec(memory_space=pltpu.VMEM)
    return pl.pallas_call(
        kernel,
        out_shape=outs,
        in_specs=[vmem] * len(args),
        out_specs=[vmem] * len(outs),
        scratch_shapes=scratch,
        compiler_params=pltpu.CompilerParams(vmem_limit_bytes=VMEM_LIMIT),
        cost_estimate=pl.CostEstimate(flops=flops, bytes_accessed=moved, transcendentals=0),
    )(*args)


def shaped(shape, dtype):
    return jax.ShapeDtypeStruct(shape, dtype)


def rolled(row, taps, shift=0):
    full = jnp.broadcast_to(row, (taps, row.shape[1]))
    return pltpu.roll(full, shift, 1, stride=1, stride_axis=0)


def index(shape, dim):
    return lax.broadcasted_iota(jnp.int32, shape, dim)


def column(row, taps):
    return jnp.broadcast_to(row, (taps, taps)).T


def prepare_kernel(
    filters_ref, signal_ref, query_ref, cot_ref, gain_ref,
    weights_ref, mirror_ref, held_ref, scaled_ref, back_taps_ref,
):
    groups, taps = filters_ref.shape
    row, col = index((taps, taps), 0), index((taps, taps), 1)
    own = row >= col
    turn = (lax.rem(row + col, taps) == 0).astype(BF16)
    back_taps_ref[...] = jnp.dot(
        filters_ref[...].astype(BF16), turn, preferred_element_type=F32
    )

    def step(g, _):
        c = rolled(back_taps_ref[pl.ds(g, 1), :], taps)
        weights_ref[g, :, :taps] = jnp.where(own, 0.0, c).astype(BF16)
        weights_ref[g, :, taps:] = jnp.where(own, c, 0.0).astype(BF16)
        return 0

    lax.fori_loop(0, groups, step, 0, unroll=4)
    swap = (row + col == taps - 1).astype(BF16)
    mirror_ref[...] = jnp.dot(swap, signal_ref[...], preferred_element_type=F32).astype(BF16)
    held_ref[...] = query_ref[...]
    scaled_ref[...] = gain_ref[...] * cot_ref[...].astype(F32)


def mix_kernel(weights_ref, before_ref, signal_ref, query_ref, scaled_ref, mixed_ref, sums_ref):
    groups, taps, _ = weights_ref.shape
    width = signal_ref.shape[1]
    per_tile = groups * LANES // width
    members = LANES // per_tile
    owner = index((taps, LANES), 1) // members

    def step(i, totals):
        lanes = pl.ds(pl.multiple_of(i * LANES, LANES), LANES)
        window = jnp.concatenate([before_ref[:, lanes], signal_ref[:, lanes]], axis=0)
        acc = None
        for k in range(per_tile):
            out = jnp.dot(weights_ref[i * per_tile + k], window, preferred_element_type=F32)
            acc = out if acc is None else jnp.where(owner == k, out, acc)
        mixed_ref[:, lanes] = acc
        lifted = query_ref[:, lanes].astype(F32) * acc
        return totals[0] + lifted * lifted, totals[1] + scaled_ref[:, lanes] * lifted

    zero = jnp.zeros((taps, LANES), F32)
    power, inner = lax.fori_loop(0, width // LANES, step, (zero, zero))
    sums = jnp.concatenate(
        [jnp.sum(power.T, axis=0, keepdims=True), jnp.sum(inner.T, axis=0, keepdims=True)], axis=0
    )
    sums_ref[...] = jnp.broadcast_to(sums[None], sums_ref.shape)


def norm_terms(sums_ref, taps):
    sums = jnp.sum(sums_ref[...], axis=0)
    recip = lax.rsqrt(sums[0:1] / D + 1e-6)
    pull = recip * recip * recip * sums[1:2] / D
    return column(recip, taps), column(pull, taps)


def filter_kernel(
    sums_ref, mixed_ref, query_ref, scaled_ref, before_ref, mirror_ref, conv_ref, totals_ref
):
    taps, width = conv_ref.shape
    pieces, per_piece, _ = totals_ref.shape
    groups = pieces * per_piece
    per_tile = groups * LANES // width
    members = LANES // per_tile
    row, col = index((taps, taps), 0), index((taps, taps), 1)
    own = row + col >= taps - 1
    swap = (row + col == taps - 1).astype(BF16)
    owner = col // members
    recip, pull = norm_terms(sums_ref, taps)

    def step(i, _):
        lanes = pl.ds(pl.multiple_of(i * LANES, LANES), LANES)
        query = query_ref[:, lanes].astype(F32)
        grad_mix = recip * scaled_ref[:, lanes] - query * mixed_ref[:, lanes] * pull
        conv = (grad_mix * query).astype(BF16)
        conv_ref[:, lanes] = conv
        past = jnp.dot(swap, before_ref[:, lanes], preferred_element_type=F32).astype(BF16)
        window = jnp.concatenate([past, mirror_ref[:, lanes]], axis=0)
        found = []
        for k in range(per_tile):
            mine = jnp.where(owner == k, conv, jnp.zeros_like(conv))
            pairs = lax.dot_general(
                mine, window, (((1,), (1,)), ((), ())), preferred_element_type=F32
            )
            both = jnp.where(own, pairs[:, taps:], pairs[:, :taps])
            lined = pltpu.roll(both, 1, 1, stride=1, stride_axis=0)
            found.append(jnp.sum(lined, axis=0, keepdims=True))
        for k in range(0, per_tile, per_piece):
            totals_ref[i * (per_tile // per_piece) + k // per_piece] = jnp.concatenate(
                found[k : k + per_piece], axis=0
            )
        return 0

    lax.fori_loop(0, width // LANES, step, 0)


def output_kernel(
    sums_ref, mixed_ref, query_ref, scaled_ref, gain_ref, normed_ref, query_grad_ref
):
    taps, width = mixed_ref.shape
    recip, pull = norm_terms(sums_ref, taps)
    for i in range(0, width, LANES):
        lanes = slice(i, i + LANES)
        mixed = mixed_ref[:, lanes]
        lifted = query_ref[:, lanes].astype(F32) * mixed
        normed_ref[:, lanes] = (lifted * recip * gain_ref[:, lanes]).astype(BF16)
        query_grad_ref[:, lanes] = (
            (recip * scaled_ref[:, lanes] - lifted * pull) * mixed
        ).astype(BF16)


def back_kernel(
    filters_ref, conv_ref, after_ref, key_ref, value_ref, key_grad_ref, value_grad_ref
):
    groups, taps = filters_ref.shape
    width = conv_ref.shape[1]
    per_tile = groups * LANES // width
    members = LANES // per_tile
    row, col = index((taps, taps), 0), index((taps, taps), 1)
    own = col >= row
    owner = col // members

    def step(i, _):
        lanes = pl.ds(pl.multiple_of(i * LANES, LANES), LANES)
        window = jnp.concatenate([conv_ref[:, lanes], after_ref[:, lanes]], axis=0)
        acc = None
        for k in range(per_tile):
            own_taps = filters_ref[pl.ds(i * per_tile + k, 1), :].astype(BF16).astype(F32)
            c = rolled(own_taps, taps)
            weights = jnp.concatenate(
                [jnp.where(own, c, 0.0).astype(BF16), jnp.where(own, 0.0, c).astype(BF16)], axis=1
            )
            out = jnp.dot(weights, window, preferred_element_type=F32)
            acc = out if acc is None else jnp.where(owner == k, out, acc)
        key_grad_ref[:, lanes] = (acc * value_ref[:, lanes].astype(F32)).astype(BF16)
        value_grad_ref[:, lanes] = (acc * key_ref[:, lanes].astype(F32)).astype(BF16)
        return 0

    lax.fori_loop(0, width // LANES, step, 0)


def gather_sum_kernel(parts_ref, out_ref):
    out_ref[...] = jnp.broadcast_to(jnp.sum(parts_ref[...], axis=0)[None], out_ref.shape)


def body(query, key_in, value_in, cotangent, filters, norm_gain):
    _, taps, width = query.shape
    groups = filters.shape[0]
    query, key_in, value_in, cotangent = (
        a.reshape(taps, width) for a in (query, key_in, value_in, cotangent)
    )
    gain = norm_gain.reshape(1, width)
    block = shaped((taps, width), BF16)
    peers = lax.axis_size("chan")
    near, far = lax.axis_size(NEAR), lax.axis_size(FAR)
    conv_flops = 4 * groups * taps * taps * LANES

    signal = (key_in.astype(F32) * value_in.astype(F32)).astype(BF16)
    before = shifted(signal, CTX, 1)
    wide = shaped((taps, width), F32)
    weights, mirror, held, scaled = call(
        prepare_kernel,
        [shaped((groups, taps, 2 * taps), BF16), block, block, wide],
        filters, signal, query, cotangent, gain,
        scratch=[pltpu.VMEM((groups, taps), F32)],
    )
    mixed, sums = call(
        mix_kernel,
        [wide, shaped((peers, 2, taps), F32)],
        weights, before, signal, held, scaled,
        flops=conv_flops,
    )
    sums = exchanged(sums, "chan")
    conv, totals = call(
        filter_kernel,
        [block, shaped((near, groups // near, taps), F32)],
        sums, mixed, held, scaled, before, mirror,
        flops=conv_flops,
    )
    totals = exchanged(totals, NEAR)
    (totals,) = call(gather_sum_kernel, [shaped((far, groups // near, taps), F32)], totals)
    totals, conv, sums = lax.optimization_barrier((totals, conv, sums))
    order = [(i + far // 2) % far for i in range(far)]
    totals = exchanged(totals, FAR, [order])
    after = shifted(conv, CTX, -1)
    normed, grad_query = call(
        output_kernel, [block, block], sums, mixed, held, scaled, gain
    )
    grad_key, grad_value = call(
        back_kernel, [block, block], filters, conv, after, key_in, value_in, flops=conv_flops
    )
    totals, normed, grad_query, grad_key, grad_value = lax.optimization_barrier(
        (totals, normed, grad_query, grad_key, grad_value)
    )
    (totals,) = call(gather_sum_kernel, [shaped((near, groups // near, taps), F32)], totals)
    grad_filters = exchanged(totals, NEAR).reshape(groups, taps)
    return tuple(a[None] for a in (normed, grad_query, grad_key, grad_value)) + (grad_filters,)


def solution(mesh):
    torus = Mesh(
        mesh.devices.reshape(8, 4, 4, mesh.shape["chan"]), ("zh", "zl", "y", "chan")
    )
    rows = P(None, CTX, "chan")
    in_specs = (rows, rows, rows, rows, P("chan", None), P("chan"))
    out_specs = (rows, rows, rows, rows, P("chan", None))

    return jax.shard_map(body, mesh=torus, in_specs=in_specs, out_specs=out_specs, check_vma=False)
```

```python
import jax
import jax.numpy as jnp
from jax import lax
from jax.experimental import pallas as pl
from jax.experimental.pallas import tpu as pltpu
from jax.sharding import Mesh
from jax.sharding import PartitionSpec as P


D = 8192
CTX = ("zh", "zl", "y")
NEAR = ("zl", "y")
FAR = "zh"
LANES = 128
VMEM_LIMIT = 16 * 2**20
F32 = jnp.float32
BF16 = jnp.bfloat16


def shifted(block, axes, distance):
    devices = range(lax.axis_size(axes))
    route = [(i - distance, i) for i in devices if i - distance in devices]
    return lax.ppermute(block, axes, route)


def exchanged(x, axes, groups=None):
    return lax.all_to_all(x, axes, 0, 0, axis_index_groups=groups, tiled=True)


def call(kernel, outs, *args, flops=0, scratch=()):
    moved = sum(a.size * a.dtype.itemsize for a in args)
    moved += sum(o.size * o.dtype.itemsize for o in outs)
    vmem = pl.BlockSpec(memory_space=pltpu.VMEM)
    return pl.pallas_call(
        kernel,
        out_shape=outs,
        in_specs=[vmem] * len(args),
        out_specs=[vmem] * len(outs),
        scratch_shapes=scratch,
        compiler_params=pltpu.CompilerParams(vmem_limit_bytes=VMEM_LIMIT),
        cost_estimate=pl.CostEstimate(flops=flops, bytes_accessed=moved, transcendentals=0),
    )(*args)


def shaped(shape, dtype):
    return jax.ShapeDtypeStruct(shape, dtype)


def rolled(row, taps, shift=0):
    full = jnp.broadcast_to(row, (taps, row.shape[1]))
    return pltpu.roll(full, shift, 1, stride=1, stride_axis=0)


def index(shape, dim):
    return lax.broadcasted_iota(jnp.int32, shape, dim)


def column(row, taps):
    return jnp.broadcast_to(row, (taps, taps)).T


def prepare_kernel(
    filters_ref, signal_ref, query_ref, cot_ref, gain_ref,
    weights_ref, mirror_ref, held_ref, scaled_ref, back_taps_ref,
):
    groups, taps = filters_ref.shape
    row, col = index((taps, taps), 0), index((taps, taps), 1)
    own = row >= col
    turn = (lax.rem(row + col, taps) == 0).astype(BF16)
    back_taps_ref[...] = jnp.dot(
        filters_ref[...].astype(BF16), turn, preferred_element_type=F32
    )

    def step(g, _):
        c = rolled(back_taps_ref[pl.ds(g, 1), :], taps)
        weights_ref[g, :, :taps] = jnp.where(own, 0.0, c).astype(BF16)
        weights_ref[g, :, taps:] = jnp.where(own, c, 0.0).astype(BF16)
        return 0

    lax.fori_loop(0, groups, step, 0, unroll=4)
    swap = (row + col == taps - 1).astype(BF16)
    mirror_ref[...] = jnp.dot(swap, signal_ref[...], preferred_element_type=F32).astype(BF16)
    held_ref[...] = query_ref[...]
    scaled_ref[...] = gain_ref[...] * cot_ref[...].astype(F32)


def mix_kernel(weights_ref, before_ref, signal_ref, query_ref, scaled_ref, mixed_ref, sums_ref):
    groups, taps, _ = weights_ref.shape
    width = signal_ref.shape[1]
    per_tile = groups * LANES // width
    members = LANES // per_tile
    owner = index((taps, LANES), 1) // members

    def step(i, totals):
        lanes = pl.ds(pl.multiple_of(i * LANES, LANES), LANES)
        window = jnp.concatenate([before_ref[:, lanes], signal_ref[:, lanes]], axis=0)
        acc = None
        for k in range(per_tile):
            out = jnp.dot(weights_ref[i * per_tile + k], window, preferred_element_type=F32)
            acc = out if acc is None else jnp.where(owner == k, out, acc)
        mixed_ref[:, lanes] = acc
        lifted = query_ref[:, lanes].astype(F32) * acc
        return totals[0] + lifted * lifted, totals[1] + scaled_ref[:, lanes] * lifted

    zero = jnp.zeros((taps, LANES), F32)
    power, inner = lax.fori_loop(0, width // LANES, step, (zero, zero))
    sums = jnp.concatenate(
        [jnp.sum(power.T, axis=0, keepdims=True), jnp.sum(inner.T, axis=0, keepdims=True)], axis=0
    )
    sums_ref[...] = jnp.broadcast_to(sums[None], sums_ref.shape)


def norm_terms(sums_ref, taps):
    sums = jnp.sum(sums_ref[...], axis=0)
    recip = lax.rsqrt(sums[0:1] / D + 1e-6)
    pull = recip * recip * recip * sums[1:2] / D
    return column(recip, taps), column(pull, taps)


def filter_kernel(
    sums_ref, mixed_ref, query_ref, scaled_ref, before_ref, mirror_ref, conv_ref, totals_ref
):
    taps, width = conv_ref.shape
    pieces, per_piece, _ = totals_ref.shape
    groups = pieces * per_piece
    per_tile = groups * LANES // width
    members = LANES // per_tile
    row, col = index((taps, taps), 0), index((taps, taps), 1)
    own = row + col >= taps - 1
    swap = (row + col == taps - 1).astype(BF16)
    owner = col // members
    recip, pull = norm_terms(sums_ref, taps)

    def step(i, _):
        lanes = pl.ds(pl.multiple_of(i * LANES, LANES), LANES)
        query = query_ref[:, lanes].astype(F32)
        grad_mix = recip * scaled_ref[:, lanes] - query * mixed_ref[:, lanes] * pull
        conv = (grad_mix * query).astype(BF16)
        conv_ref[:, lanes] = conv
        past = jnp.dot(swap, before_ref[:, lanes], preferred_element_type=F32).astype(BF16)
        window = jnp.concatenate([past, mirror_ref[:, lanes]], axis=0)
        found = []
        for k in range(per_tile):
            mine = jnp.where(owner == k, conv, jnp.zeros_like(conv))
            pairs = lax.dot_general(
                mine, window, (((1,), (1,)), ((), ())), preferred_element_type=F32
            )
            both = jnp.where(own, pairs[:, taps:], pairs[:, :taps])
            lined = pltpu.roll(both, 1, 1, stride=1, stride_axis=0)
            found.append(jnp.sum(lined, axis=0, keepdims=True))
        for k in range(0, per_tile, per_piece):
            totals_ref[i * (per_tile // per_piece) + k // per_piece] = jnp.concatenate(
                found[k : k + per_piece], axis=0
            )
        return 0

    lax.fori_loop(0, width // LANES, step, 0)


def output_kernel(
    sums_ref, mixed_ref, query_ref, scaled_ref, gain_ref, normed_ref, query_grad_ref
):
    taps, width = mixed_ref.shape
    recip, pull = norm_terms(sums_ref, taps)
    for i in range(0, width, LANES):
        lanes = slice(i, i + LANES)
        mixed = mixed_ref[:, lanes]
        lifted = query_ref[:, lanes].astype(F32) * mixed
        normed_ref[:, lanes] = (lifted * recip * gain_ref[:, lanes]).astype(BF16)
        query_grad_ref[:, lanes] = (
            (recip * scaled_ref[:, lanes] - lifted * pull) * mixed
        ).astype(BF16)


def back_kernel(
    filters_ref, conv_ref, after_ref, key_ref, value_ref, key_grad_ref, value_grad_ref
):
    groups, taps = filters_ref.shape
    width = conv_ref.shape[1]
    per_tile = groups * LANES // width
    members = LANES // per_tile
    row, col = index((taps, taps), 0), index((taps, taps), 1)
    own = col >= row
    owner = col // members

    def step(i, _):
        lanes = pl.ds(pl.multiple_of(i * LANES, LANES), LANES)
        window = jnp.concatenate([conv_ref[:, lanes], after_ref[:, lanes]], axis=0)
        acc = None
        for k in range(per_tile):
            own_taps = filters_ref[pl.ds(i * per_tile + k, 1), :].astype(BF16).astype(F32)
            c = rolled(own_taps, taps)
            weights = jnp.concatenate(
                [jnp.where(own, c, 0.0).astype(BF16), jnp.where(own, 0.0, c).astype(BF16)], axis=1
            )
            out = jnp.dot(weights, window, preferred_element_type=F32)
            acc = out if acc is None else jnp.where(owner == k, out, acc)
        key_grad_ref[:, lanes] = (acc * value_ref[:, lanes].astype(F32)).astype(BF16)
        value_grad_ref[:, lanes] = (acc * key_ref[:, lanes].astype(F32)).astype(BF16)
        return 0

    lax.fori_loop(0, width // LANES, step, 0)


def gather_sum_kernel(parts_ref, out_ref):
    out_ref[...] = jnp.broadcast_to(jnp.sum(parts_ref[...], axis=0)[None], out_ref.shape)


def body(query, key_in, value_in, cotangent, filters, norm_gain):
    _, taps, width = query.shape
    groups = filters.shape[0]
    query, key_in, value_in, cotangent = (
        a.reshape(taps, width) for a in (query, key_in, value_in, cotangent)
    )
    gain = norm_gain.reshape(1, width)
    block = shaped((taps, width), BF16)
    peers = lax.axis_size("chan")
    near, far = lax.axis_size(NEAR), lax.axis_size(FAR)
    conv_flops = 4 * groups * taps * taps * LANES

    signal = (key_in.astype(F32) * value_in.astype(F32)).astype(BF16)
    before = shifted(signal, CTX, 1)
    wide = shaped((taps, width), F32)
    weights, mirror, held, scaled = call(
        prepare_kernel,
        [shaped((groups, taps, 2 * taps), BF16), block, block, wide],
        filters, signal, query, cotangent, gain,
        scratch=[pltpu.VMEM((groups, taps), F32)],
    )
    mixed, sums = call(
        mix_kernel,
        [wide, shaped((peers, 2, taps), F32)],
        weights, before, signal, held, scaled,
        flops=conv_flops,
    )
    sums = exchanged(sums, "chan")
    conv, totals = call(
        filter_kernel,
        [block, shaped((near, groups // near, taps), F32)],
        sums, mixed, held, scaled, before, mirror,
        flops=conv_flops,
    )
    totals = exchanged(totals, NEAR)
    after = shifted(conv, CTX, -1)
    normed, grad_query = call(
        output_kernel, [block, block], sums, mixed, held, scaled, gain
    )
    totals, normed, grad_query = lax.optimization_barrier((totals, normed, grad_query))
    (totals,) = call(gather_sum_kernel, [shaped((far, groups // near, taps), F32)], totals)
    order = [(i + far // 2) % far for i in range(far)]
    totals = exchanged(totals, FAR, [order])
    (totals,) = call(gather_sum_kernel, [shaped((near, groups // near, taps), F32)], totals)
    grad_filters = exchanged(totals, NEAR).reshape(groups, taps)
    grad_key, grad_value = call(
        back_kernel, [block, block], filters, conv, after, key_in, value_in,
        flops=conv_flops,
    )
    return tuple(a[None] for a in (normed, grad_query, grad_key, grad_value)) + (grad_filters,)


def solution(mesh):
    torus = Mesh(
        mesh.devices.reshape(8, 4, 4, mesh.shape["chan"]), ("zh", "zl", "y", "chan")
    )
    rows = P(None, CTX, "chan")
    in_specs = (rows, rows, rows, rows, P("chan", None), P("chan"))
    out_specs = (rows, rows, rows, rows, P("chan", None))

    return jax.shard_map(body, mesh=torus, in_specs=in_specs, out_specs=out_specs, check_vma=False)
```

```python
import math

import jax
import jax.numpy as jnp
from jax import lax
from jax.experimental import pallas as pl
from jax.experimental.pallas import tpu as pltpu
from jax.sharding import Mesh
from jax.sharding import PartitionSpec as P


D = 8192
CTX = ("zh", "zl", "y")
NEAR = ("zl", "y")
FAR = "zh"
LANES = 128
VMEM_LIMIT = 16 * 2**20
F32 = jnp.float32
BF16 = jnp.bfloat16


def shifted(block, axes, distance):
    devices = range(lax.axis_size(axes))
    route = [(i - distance, i) for i in devices if i - distance in devices]
    return lax.ppermute(block, axes, route)


def exchanged(x, axes, groups=None):
    return lax.all_to_all(x, axes, 0, 0, axis_index_groups=groups, tiled=True)


def call(kernel, outs, *args, flops=0, scratch=(), outside=()):
    moved = sum(a.size * a.dtype.itemsize for a in args)
    moved += sum(math.prod(o.shape) * o.dtype.itemsize for o in outs)
    vmem = pl.BlockSpec(memory_space=pltpu.VMEM)
    hbm = pl.BlockSpec(memory_space=pltpu.HBM)
    args = [
        pltpu.with_memory_space_constraint(a, pltpu.HBM) if i in outside else a
        for i, a in enumerate(args)
    ]
    return pl.pallas_call(
        kernel,
        out_shape=outs,
        in_specs=[hbm if i in outside else vmem for i in range(len(args))],
        out_specs=[vmem] * len(outs),
        scratch_shapes=scratch,
        compiler_params=pltpu.CompilerParams(vmem_limit_bytes=VMEM_LIMIT),
        cost_estimate=pl.CostEstimate(flops=flops, bytes_accessed=moved, transcendentals=0),
    )(*args)


def shaped(shape, dtype):
    return jax.ShapeDtypeStruct(shape, dtype)


def rolled(row, taps, shift=0):
    full = jnp.broadcast_to(row, (taps, row.shape[1]))
    return pltpu.roll(full, shift, 1, stride=1, stride_axis=0)


def index(shape, dim):
    return lax.broadcasted_iota(jnp.int32, shape, dim)


def column(row, taps):
    return jnp.broadcast_to(row, (taps, taps)).T


def prepare_kernel(
    filters_ref, signal_ref, query_ref, cot_ref, gain_ref,
    weights_ref, mirror_ref, held_ref, scaled_ref, taps_ref, back_taps_ref, cot_copy, gain_copy, sems,
):
    groups, taps = filters_ref.shape
    copies = [
        pltpu.make_async_copy(source, target, sems.at[i])
        for i, (source, target) in enumerate(
            [(filters_ref, taps_ref), (gain_ref, gain_copy), (cot_ref, cot_copy), (query_ref, held_ref)]
        )
    ]
    for copy in copies:
        copy.start()
    row, col = index((taps, taps), 0), index((taps, taps), 1)
    swap = (row + col == taps - 1).astype(BF16)
    mirror_ref[...] = jnp.dot(swap, signal_ref[...], preferred_element_type=F32).astype(BF16)
    copies[0].wait()
    own = row >= col
    turn = (lax.rem(row + col, taps) == 0).astype(BF16)
    back_taps_ref[...] = jnp.dot(
        taps_ref[...].astype(BF16), turn, preferred_element_type=F32
    )

    def step(g, _):
        c = rolled(back_taps_ref[pl.ds(g, 1), :], taps)
        weights_ref[g, :, :taps] = jnp.where(own, 0.0, c).astype(BF16)
        weights_ref[g, :, taps:] = jnp.where(own, c, 0.0).astype(BF16)
        return 0

    lax.fori_loop(0, groups, step, 0, unroll=4)
    for copy in copies[1:]:
        copy.wait()
    scaled_ref[...] = gain_copy[...] * cot_copy[...].astype(F32)


def mix_kernel(weights_ref, before_ref, signal_ref, query_ref, scaled_ref, mixed_ref, sums_ref):
    groups, taps, _ = weights_ref.shape
    width = signal_ref.shape[1]
    per_tile = groups * LANES // width
    members = LANES // per_tile
    owner = index((taps, LANES), 1) // members

    def step(i, totals):
        lanes = pl.ds(pl.multiple_of(i * LANES, LANES), LANES)
        window = jnp.concatenate([before_ref[:, lanes], signal_ref[:, lanes]], axis=0)
        acc = None
        for k in range(per_tile):
            out = jnp.dot(weights_ref[i * per_tile + k], window, preferred_element_type=F32)
            acc = out if acc is None else jnp.where(owner == k, out, acc)
        mixed_ref[:, lanes] = acc
        lifted = query_ref[:, lanes].astype(F32) * acc
        return totals[0] + lifted * lifted, totals[1] + scaled_ref[:, lanes] * lifted

    zero = jnp.zeros((taps, LANES), F32)
    power, inner = lax.fori_loop(0, width // LANES, step, (zero, zero))
    sums = jnp.concatenate(
        [jnp.sum(power.T, axis=0, keepdims=True), jnp.sum(inner.T, axis=0, keepdims=True)], axis=0
    )
    sums_ref[...] = jnp.broadcast_to(sums[None], sums_ref.shape)


def norm_terms(sums_ref, taps):
    sums = jnp.sum(sums_ref[...], axis=0)
    recip = lax.rsqrt(sums[0:1] / D + 1e-6)
    pull = recip * recip * recip * sums[1:2] / D
    return column(recip, taps), column(pull, taps)


def filter_kernel(
    sums_ref, mixed_ref, query_ref, scaled_ref, before_ref, mirror_ref, conv_ref, totals_ref
):
    taps, width = conv_ref.shape
    pieces, per_piece, _ = totals_ref.shape
    groups = pieces * per_piece
    per_tile = groups * LANES // width
    members = LANES // per_tile
    row, col = index((taps, taps), 0), index((taps, taps), 1)
    own = row + col >= taps - 1
    swap = (row + col == taps - 1).astype(BF16)
    owner = col // members
    recip, pull = norm_terms(sums_ref, taps)

    def step(i, _):
        lanes = pl.ds(pl.multiple_of(i * LANES, LANES), LANES)
        query = query_ref[:, lanes].astype(F32)
        grad_mix = recip * scaled_ref[:, lanes] - query * mixed_ref[:, lanes] * pull
        conv = (grad_mix * query).astype(BF16)
        conv_ref[:, lanes] = conv
        past = jnp.dot(swap, before_ref[:, lanes], preferred_element_type=F32).astype(BF16)
        window = jnp.concatenate([past, mirror_ref[:, lanes]], axis=0)
        found = []
        for k in range(per_tile):
            mine = jnp.where(owner == k, conv, jnp.zeros_like(conv))
            pairs = lax.dot_general(
                mine, window, (((1,), (1,)), ((), ())), preferred_element_type=F32
            )
            both = jnp.where(own, pairs[:, taps:], pairs[:, :taps])
            lined = pltpu.roll(both, 1, 1, stride=1, stride_axis=0)
            found.append(jnp.sum(lined, axis=0, keepdims=True))
        for k in range(0, per_tile, per_piece):
            totals_ref[i * (per_tile // per_piece) + k // per_piece] = jnp.concatenate(
                found[k : k + per_piece], axis=0
            )
        return 0

    lax.fori_loop(0, width // LANES, step, 0)


def output_kernel(
    sums_ref, mixed_ref, query_ref, scaled_ref, gain_ref, normed_ref, query_grad_ref
):
    taps, width = mixed_ref.shape
    recip, pull = norm_terms(sums_ref, taps)
    for i in range(0, width, LANES):
        lanes = slice(i, i + LANES)
        mixed = mixed_ref[:, lanes]
        lifted = query_ref[:, lanes].astype(F32) * mixed
        normed_ref[:, lanes] = (lifted * recip * gain_ref[:, lanes]).astype(BF16)
        query_grad_ref[:, lanes] = (
            (recip * scaled_ref[:, lanes] - lifted * pull) * mixed
        ).astype(BF16)


def back_kernel(
    filters_ref, conv_ref, after_ref, key_ref, value_ref, key_grad_ref, value_grad_ref
):
    groups, taps = filters_ref.shape
    width = conv_ref.shape[1]
    per_tile = groups * LANES // width
    members = LANES // per_tile
    row, col = index((taps, taps), 0), index((taps, taps), 1)
    own = col >= row
    owner = col // members

    def step(i, _):
        lanes = pl.ds(pl.multiple_of(i * LANES, LANES), LANES)
        window = jnp.concatenate([conv_ref[:, lanes], after_ref[:, lanes]], axis=0)
        acc = None
        for k in range(per_tile):
            own_taps = filters_ref[pl.ds(i * per_tile + k, 1), :].astype(BF16).astype(F32)
            c = rolled(own_taps, taps)
            weights = jnp.concatenate(
                [jnp.where(own, c, 0.0).astype(BF16), jnp.where(own, 0.0, c).astype(BF16)], axis=1
            )
            out = jnp.dot(weights, window, preferred_element_type=F32)
            acc = out if acc is None else jnp.where(owner == k, out, acc)
        key_grad_ref[:, lanes] = (acc * value_ref[:, lanes].astype(F32)).astype(BF16)
        value_grad_ref[:, lanes] = (acc * key_ref[:, lanes].astype(F32)).astype(BF16)
        return 0

    lax.fori_loop(0, width // LANES, step, 0)


def gather_sum_kernel(parts_ref, out_ref):
    out_ref[...] = jnp.broadcast_to(jnp.sum(parts_ref[...], axis=0)[None], out_ref.shape)


def body(query, key_in, value_in, cotangent, filters, norm_gain):
    _, taps, width = query.shape
    groups = filters.shape[0]
    query, key_in, value_in, cotangent = (
        a.reshape(taps, width) for a in (query, key_in, value_in, cotangent)
    )
    gain = norm_gain.reshape(1, width)
    block = shaped((taps, width), BF16)
    peers = lax.axis_size("chan")
    near, far = lax.axis_size(NEAR), lax.axis_size(FAR)
    conv_flops = 4 * groups * taps * taps * LANES

    signal = (key_in.astype(F32) * value_in.astype(F32)).astype(BF16)
    before = shifted(signal, CTX, 1)
    wide = shaped((taps, width), F32)
    weights, mirror, held, scaled = call(
        prepare_kernel,
        [shaped((groups, taps, 2 * taps), BF16), block, block, wide],
        filters, signal, query, cotangent, gain,
        scratch=[
            pltpu.VMEM((groups, taps), F32),
            pltpu.VMEM((groups, taps), F32),
            pltpu.VMEM((taps, width), BF16),
            pltpu.VMEM((1, width), F32),
            pltpu.SemaphoreType.DMA((4,)),
        ],
        outside=(0, 2, 3, 4),
    )
    mixed, sums = call(
        mix_kernel,
        [wide, shaped((peers, 2, taps), F32)],
        weights, before, signal, held, scaled,
        flops=conv_flops,
    )
    sums = exchanged(sums, "chan")
    conv, totals = call(
        filter_kernel,
        [block, shaped((near, groups // near, taps), F32)],
        sums, mixed, held, scaled, before, mirror,
        flops=conv_flops,
    )
    totals = exchanged(totals, NEAR)
    (totals,) = call(gather_sum_kernel, [shaped((far, groups // near, taps), F32)], totals)
    order = [(i + far // 2) % far for i in range(far)]
    totals = exchanged(totals, FAR, [order])
    after = shifted(conv, CTX, -1)
    (totals,) = call(gather_sum_kernel, [shaped((near, groups // near, taps), F32)], totals)
    grad_filters = exchanged(totals, NEAR).reshape(groups, taps)
    normed, grad_query = call(
        output_kernel, [block, block], sums, mixed, held, scaled, gain
    )
    after, normed, grad_query = lax.optimization_barrier((after, normed, grad_query))
    grad_key, grad_value = call(
        back_kernel, [block, block], filters, conv, after, key_in, value_in,
        flops=conv_flops,
    )
    return tuple(a[None] for a in (normed, grad_query, grad_key, grad_value)) + (grad_filters,)


def solution(mesh):
    torus = Mesh(
        mesh.devices.reshape(8, 4, 4, mesh.shape["chan"]), ("zh", "zl", "y", "chan")
    )
    rows = P(None, CTX, "chan")
    in_specs = (rows, rows, rows, rows, P("chan", None), P("chan"))
    out_specs = (rows, rows, rows, rows, P("chan", None))

    return jax.shard_map(body, mesh=torus, in_specs=in_specs, out_specs=out_specs, check_vma=False)
```

```python
import math

import jax
import jax.numpy as jnp
from jax import lax
from jax.experimental import pallas as pl
from jax.experimental.pallas import tpu as pltpu
from jax.sharding import Mesh
from jax.sharding import PartitionSpec as P


D = 8192
CTX = ("far", "near")
LANES = 128
VMEM_LIMIT = 16 * 2**20
F32 = jnp.float32
BF16 = jnp.bfloat16


def shifted(block, axes, distance):
    devices = range(lax.axis_size(axes))
    route = [(i - distance, i) for i in devices if i - distance in devices]
    return lax.ppermute(block, axes, route)


def exchanged(x, axis, first=0):
    size = lax.axis_size(axis)
    order = [(i + first) % size for i in range(size)]
    return lax.all_to_all(x, axis, 0, 0, axis_index_groups=[order], tiled=True)


def call(kernel, outs, *args, flops=0, scratch=(), outside=()):
    moved = sum(a.size * a.dtype.itemsize for a in args)
    moved += sum(math.prod(o.shape) * o.dtype.itemsize for o in outs)
    vmem = pl.BlockSpec(memory_space=pltpu.VMEM)
    hbm = pl.BlockSpec(memory_space=pltpu.HBM)
    args = [
        pltpu.with_memory_space_constraint(a, pltpu.HBM) if i in outside else a
        for i, a in enumerate(args)
    ]
    return pl.pallas_call(
        kernel,
        out_shape=outs,
        in_specs=[hbm if i in outside else vmem for i in range(len(args))],
        out_specs=[vmem] * len(outs),
        scratch_shapes=scratch,
        compiler_params=pltpu.CompilerParams(vmem_limit_bytes=VMEM_LIMIT),
        cost_estimate=pl.CostEstimate(flops=flops, bytes_accessed=moved, transcendentals=0),
    )(*args)


def shaped(shape, dtype):
    return jax.ShapeDtypeStruct(shape, dtype)


def rolled(row, taps, shift=0):
    full = jnp.broadcast_to(row, (taps, row.shape[1]))
    return pltpu.roll(full, shift, 1, stride=1, stride_axis=0)


def index(shape, dim):
    return lax.broadcasted_iota(jnp.int32, shape, dim)


def column(row, taps):
    return jnp.broadcast_to(row, (taps, taps)).T


def prepare_kernel(
    filters_ref, signal_ref, query_ref, cot_ref, gain_ref,
    weights_ref, mirror_ref, held_ref, scaled_ref, taps_ref, back_taps_ref, cot_copy, gain_copy, sems,
):
    groups, taps = filters_ref.shape
    copies = [
        pltpu.make_async_copy(source, target, sems.at[i])
        for i, (source, target) in enumerate(
            [(filters_ref, taps_ref), (gain_ref, gain_copy), (cot_ref, cot_copy), (query_ref, held_ref)]
        )
    ]
    for copy in copies:
        copy.start()
    row, col = index((taps, taps), 0), index((taps, taps), 1)
    swap = (row + col == taps - 1).astype(BF16)
    mirror_ref[...] = jnp.dot(swap, signal_ref[...], preferred_element_type=F32).astype(BF16)
    copies[0].wait()
    own = row >= col
    turn = (lax.rem(row + col, taps) == 0).astype(BF16)
    back_taps_ref[...] = jnp.dot(
        taps_ref[...].astype(BF16), turn, preferred_element_type=F32
    )

    def step(g, _):
        c = rolled(back_taps_ref[pl.ds(g, 1), :], taps)
        weights_ref[g, :, :taps] = jnp.where(own, 0.0, c).astype(BF16)
        weights_ref[g, :, taps:] = jnp.where(own, c, 0.0).astype(BF16)
        return 0

    lax.fori_loop(0, groups, step, 0, unroll=4)
    for copy in copies[1:]:
        copy.wait()
    scaled_ref[...] = gain_copy[...] * cot_copy[...].astype(F32)


def mix_kernel(weights_ref, before_ref, signal_ref, query_ref, scaled_ref, mixed_ref, sums_ref):
    groups, taps, _ = weights_ref.shape
    width = signal_ref.shape[1]
    per_tile = groups * LANES // width
    members = LANES // per_tile
    owner = index((taps, LANES), 1) // members

    def step(i, totals):
        lanes = pl.ds(pl.multiple_of(i * LANES, LANES), LANES)
        window = jnp.concatenate([before_ref[:, lanes], signal_ref[:, lanes]], axis=0)
        acc = None
        for k in range(per_tile):
            out = jnp.dot(weights_ref[i * per_tile + k], window, preferred_element_type=F32)
            acc = out if acc is None else jnp.where(owner == k, out, acc)
        mixed_ref[:, lanes] = acc
        lifted = query_ref[:, lanes].astype(F32) * acc
        return totals[0] + lifted * lifted, totals[1] + scaled_ref[:, lanes] * lifted

    zero = jnp.zeros((taps, LANES), F32)
    power, inner = lax.fori_loop(0, width // LANES, step, (zero, zero))
    sums = jnp.concatenate(
        [jnp.sum(power.T, axis=0, keepdims=True), jnp.sum(inner.T, axis=0, keepdims=True)], axis=0
    )
    sums_ref[...] = jnp.broadcast_to(sums[None], sums_ref.shape)


def norm_terms(sums_ref, taps):
    sums = jnp.sum(sums_ref[...], axis=0)
    recip = lax.rsqrt(sums[0:1] / D + 1e-6)
    pull = recip * recip * recip * sums[1:2] / D
    return column(recip, taps), column(pull, taps)


def filter_kernel(
    sums_ref, mixed_ref, query_ref, scaled_ref, before_ref, mirror_ref, conv_ref, totals_ref
):
    taps, width = conv_ref.shape
    pieces, per_piece, _ = totals_ref.shape
    groups = pieces * per_piece
    per_tile = groups * LANES // width
    members = LANES // per_tile
    row, col = index((taps, taps), 0), index((taps, taps), 1)
    own = row + col >= taps - 1
    swap = (row + col == taps - 1).astype(BF16)
    owner = col // members
    recip, pull = norm_terms(sums_ref, taps)

    def step(i, _):
        lanes = pl.ds(pl.multiple_of(i * LANES, LANES), LANES)
        query = query_ref[:, lanes].astype(F32)
        grad_mix = recip * scaled_ref[:, lanes] - query * mixed_ref[:, lanes] * pull
        conv = (grad_mix * query).astype(BF16)
        conv_ref[:, lanes] = conv
        past = jnp.dot(swap, before_ref[:, lanes], preferred_element_type=F32).astype(BF16)
        window = jnp.concatenate([past, mirror_ref[:, lanes]], axis=0)
        found = []
        for k in range(per_tile):
            mine = jnp.where(owner == k, conv, jnp.zeros_like(conv))
            pairs = lax.dot_general(
                mine, window, (((1,), (1,)), ((), ())), preferred_element_type=F32
            )
            both = jnp.where(own, pairs[:, taps:], pairs[:, :taps])
            lined = pltpu.roll(both, 1, 1, stride=1, stride_axis=0)
            found.append(jnp.sum(lined, axis=0, keepdims=True))
        for k in range(0, per_tile, per_piece):
            totals_ref[i * (per_tile // per_piece) + k // per_piece] = jnp.concatenate(
                found[k : k + per_piece], axis=0
            )
        return 0

    lax.fori_loop(0, width // LANES, step, 0)


def output_kernel(
    sums_ref, mixed_ref, query_ref, scaled_ref, gain_ref, normed_ref, query_grad_ref
):
    taps, width = mixed_ref.shape
    recip, pull = norm_terms(sums_ref, taps)
    for i in range(0, width, LANES):
        lanes = slice(i, i + LANES)
        mixed = mixed_ref[:, lanes]
        lifted = query_ref[:, lanes].astype(F32) * mixed
        normed_ref[:, lanes] = (lifted * recip * gain_ref[:, lanes]).astype(BF16)
        query_grad_ref[:, lanes] = (
            (recip * scaled_ref[:, lanes] - lifted * pull) * mixed
        ).astype(BF16)


def back_kernel(
    filters_ref, conv_ref, after_ref, key_ref, value_ref, key_grad_ref, value_grad_ref
):
    groups, taps = filters_ref.shape
    width = conv_ref.shape[1]
    per_tile = groups * LANES // width
    members = LANES // per_tile
    row, col = index((taps, taps), 0), index((taps, taps), 1)
    own = col >= row
    owner = col // members

    def step(i, _):
        lanes = pl.ds(pl.multiple_of(i * LANES, LANES), LANES)
        window = jnp.concatenate([conv_ref[:, lanes], after_ref[:, lanes]], axis=0)
        acc = None
        for k in range(per_tile):
            own_taps = filters_ref[pl.ds(i * per_tile + k, 1), :].astype(BF16).astype(F32)
            c = rolled(own_taps, taps)
            weights = jnp.concatenate(
                [jnp.where(own, c, 0.0).astype(BF16), jnp.where(own, 0.0, c).astype(BF16)], axis=1
            )
            out = jnp.dot(weights, window, preferred_element_type=F32)
            acc = out if acc is None else jnp.where(owner == k, out, acc)
        key_grad_ref[:, lanes] = (acc * value_ref[:, lanes].astype(F32)).astype(BF16)
        value_grad_ref[:, lanes] = (acc * key_ref[:, lanes].astype(F32)).astype(BF16)
        return 0

    lax.fori_loop(0, width // LANES, step, 0)


def gather_sum_kernel(parts_ref, out_ref):
    out_ref[...] = jnp.broadcast_to(jnp.sum(parts_ref[...], axis=0)[None], out_ref.shape)


def body(query, key_in, value_in, cotangent, filters, norm_gain):
    _, taps, width = query.shape
    groups = filters.shape[0]
    query, key_in, value_in, cotangent = (
        a.reshape(taps, width) for a in (query, key_in, value_in, cotangent)
    )
    gain = norm_gain.reshape(1, width)
    block = shaped((taps, width), BF16)
    peers = lax.axis_size("chan")
    near, far = lax.axis_size("near"), lax.axis_size("far")
    conv_flops = 4 * groups * taps * taps * LANES

    signal = (key_in.astype(F32) * value_in.astype(F32)).astype(BF16)
    before = shifted(signal, CTX, 1)
    wide = shaped((taps, width), F32)
    weights, mirror, held, scaled = call(
        prepare_kernel,
        [shaped((groups, taps, 2 * taps), BF16), block, block, wide],
        filters, signal, query, cotangent, gain,
        scratch=[
            pltpu.VMEM((groups, taps), F32),
            pltpu.VMEM((groups, taps), F32),
            pltpu.VMEM((taps, width), BF16),
            pltpu.VMEM((1, width), F32),
            pltpu.SemaphoreType.DMA((4,)),
        ],
        outside=(0, 2, 3, 4),
    )
    mixed, sums = call(
        mix_kernel,
        [wide, shaped((peers, 2, taps), F32)],
        weights, before, signal, held, scaled,
        flops=conv_flops,
    )
    sums = exchanged(sums, "chan")
    conv, totals = call(
        filter_kernel,
        [block, shaped((near, groups // near, taps), F32)],
        sums, mixed, held, scaled, before, mirror,
        flops=conv_flops,
    )
    totals = exchanged(totals, "near", near // 4)
    (totals,) = call(gather_sum_kernel, [shaped((far, groups // near, taps), F32)], totals)
    totals = exchanged(totals, "far", far // 2)
    after = shifted(conv, CTX, -1)
    (totals,) = call(gather_sum_kernel, [shaped((near, groups // near, taps), F32)], totals)
    grad_filters = exchanged(totals, "near", near // 4).reshape(groups, taps)
    normed, grad_query = call(
        output_kernel, [block, block], sums, mixed, held, scaled, gain
    )
    after, normed, grad_query = lax.optimization_barrier((after, normed, grad_query))
    grad_key, grad_value = call(
        back_kernel, [block, block], filters, conv, after, key_in, value_in,
        flops=conv_flops,
    )
    return tuple(a[None] for a in (normed, grad_query, grad_key, grad_value)) + (grad_filters,)


def solution(mesh):
    torus = Mesh(
        mesh.devices.reshape(8, 16, mesh.shape["chan"]), ("far", "near", "chan")
    )
    rows = P(None, CTX, "chan")
    in_specs = (rows, rows, rows, rows, P("chan", None), P("chan"))
    out_specs = (rows, rows, rows, rows, P("chan", None))

    return jax.shard_map(body, mesh=torus, in_specs=in_specs, out_specs=out_specs, check_vma=False)
```

```python
import math

import jax
import jax.numpy as jnp
from jax import lax
from jax.experimental import pallas as pl
from jax.experimental.pallas import tpu as pltpu
from jax.sharding import Mesh
from jax.sharding import PartitionSpec as P


D = 8192
CTX = ("far", "near")
LANES = 128
VMEM_LIMIT = 16 * 2**20
F32 = jnp.float32
BF16 = jnp.bfloat16


def shifted(block, axes, distance):
    devices = range(lax.axis_size(axes))
    route = [(i - distance, i) for i in devices if i - distance in devices]
    return lax.ppermute(block, axes, route)


def exchanged(x, axis, first=0):
    size = lax.axis_size(axis)
    order = [[(i + first) % size for i in range(size)]] if first else None
    return lax.all_to_all(x, axis, 0, 0, axis_index_groups=order, tiled=True)


def call(kernel, outs, *args, flops=0, scratch=(), outside=()):
    moved = sum(a.size * a.dtype.itemsize for a in args)
    moved += sum(math.prod(o.shape) * o.dtype.itemsize for o in outs)
    vmem = pl.BlockSpec(memory_space=pltpu.VMEM)
    hbm = pl.BlockSpec(memory_space=pltpu.HBM)
    args = [
        pltpu.with_memory_space_constraint(a, pltpu.HBM) if i in outside else a
        for i, a in enumerate(args)
    ]
    return pl.pallas_call(
        kernel,
        out_shape=outs,
        in_specs=[hbm if i in outside else vmem for i in range(len(args))],
        out_specs=[vmem] * len(outs),
        scratch_shapes=scratch,
        compiler_params=pltpu.CompilerParams(vmem_limit_bytes=VMEM_LIMIT),
        cost_estimate=pl.CostEstimate(flops=flops, bytes_accessed=moved, transcendentals=0),
    )(*args)


def shaped(shape, dtype):
    return jax.ShapeDtypeStruct(shape, dtype)


def rolled(row, taps, shift=0):
    full = jnp.broadcast_to(row, (taps, row.shape[1]))
    return pltpu.roll(full, shift, 1, stride=1, stride_axis=0)


def index(shape, dim):
    return lax.broadcasted_iota(jnp.int32, shape, dim)


def column(row, taps):
    return jnp.broadcast_to(row, (taps, taps)).T


def prepare_kernel(
    filters_ref, signal_ref, query_ref, cot_ref, gain_ref,
    weights_ref, mirror_ref, held_ref, scaled_ref, taps_ref, back_taps_ref, cot_copy, gain_copy, sems,
):
    groups, taps = filters_ref.shape
    copies = [
        pltpu.make_async_copy(source, target, sems.at[i])
        for i, (source, target) in enumerate(
            [(filters_ref, taps_ref), (gain_ref, gain_copy), (cot_ref, cot_copy), (query_ref, held_ref)]
        )
    ]
    for copy in copies:
        copy.start()
    row, col = index((taps, taps), 0), index((taps, taps), 1)
    swap = (row + col == taps - 1).astype(BF16)
    mirror_ref[...] = jnp.dot(swap, signal_ref[...], preferred_element_type=F32).astype(BF16)
    copies[0].wait()
    own = row >= col
    turn = (lax.rem(row + col, taps) == 0).astype(BF16)
    back_taps_ref[...] = jnp.dot(
        taps_ref[...].astype(BF16), turn, preferred_element_type=F32
    )

    def step(g, _):
        c = rolled(back_taps_ref[pl.ds(g, 1), :], taps)
        weights_ref[g, :, :taps] = jnp.where(own, 0.0, c).astype(BF16)
        weights_ref[g, :, taps:] = jnp.where(own, c, 0.0).astype(BF16)
        return 0

    lax.fori_loop(0, groups, step, 0, unroll=8)
    for copy in copies[1:]:
        copy.wait()
    scaled_ref[...] = gain_copy[...] * cot_copy[...].astype(F32)


def mix_kernel(weights_ref, before_ref, signal_ref, query_ref, scaled_ref, mixed_ref, sums_ref):
    groups, taps, _ = weights_ref.shape
    width = signal_ref.shape[1]
    per_tile = groups * LANES // width
    members = LANES // per_tile
    owner = index((taps, LANES), 1) // members

    def step(i, totals):
        lanes = pl.ds(pl.multiple_of(i * LANES, LANES), LANES)
        window = jnp.concatenate([before_ref[:, lanes], signal_ref[:, lanes]], axis=0)
        acc = None
        for k in range(per_tile):
            out = jnp.dot(weights_ref[i * per_tile + k], window, preferred_element_type=F32)
            acc = out if acc is None else jnp.where(owner == k, out, acc)
        mixed_ref[:, lanes] = acc
        lifted = query_ref[:, lanes].astype(F32) * acc
        return totals[0] + lifted * lifted, totals[1] + scaled_ref[:, lanes] * lifted

    zero = jnp.zeros((taps, LANES), F32)
    power, inner = lax.fori_loop(0, width // LANES, step, (zero, zero), unroll=8)
    sums = jnp.concatenate(
        [jnp.sum(power.T, axis=0, keepdims=True), jnp.sum(inner.T, axis=0, keepdims=True)], axis=0
    )
    sums_ref[...] = jnp.broadcast_to(sums[None], sums_ref.shape)


def norm_terms(sums_ref, taps):
    sums = jnp.sum(sums_ref[...], axis=0)
    recip = lax.rsqrt(sums[0:1] / D + 1e-6)
    pull = recip * recip * recip * sums[1:2] / D
    return column(recip, taps), column(pull, taps)


def filter_kernel(
    sums_ref, mixed_ref, query_ref, scaled_ref, before_ref, mirror_ref, conv_ref, totals_ref
):
    taps, width = conv_ref.shape
    pieces, per_piece, _ = totals_ref.shape
    groups = pieces * per_piece
    per_tile = groups * LANES // width
    members = LANES // per_tile
    row, col = index((taps, taps), 0), index((taps, taps), 1)
    own = row + col >= taps - 1
    swap = (row + col == taps - 1).astype(BF16)
    owner = col // members
    recip, pull = norm_terms(sums_ref, taps)

    def step(i, _):
        lanes = pl.ds(pl.multiple_of(i * LANES, LANES), LANES)
        query = query_ref[:, lanes].astype(F32)
        grad_mix = recip * scaled_ref[:, lanes] - query * mixed_ref[:, lanes] * pull
        conv = (grad_mix * query).astype(BF16)
        conv_ref[:, lanes] = conv
        past = jnp.dot(swap, before_ref[:, lanes], preferred_element_type=F32).astype(BF16)
        window = jnp.concatenate([past, mirror_ref[:, lanes]], axis=0)
        found = []
        for k in range(per_tile):
            mine = jnp.where(owner == k, conv, jnp.zeros_like(conv))
            pairs = lax.dot_general(
                mine, window, (((1,), (1,)), ((), ())), preferred_element_type=F32
            )
            both = jnp.where(own, pairs[:, taps:], pairs[:, :taps])
            lined = pltpu.roll(both, 1, 1, stride=1, stride_axis=0)
            found.append(jnp.sum(lined, axis=0, keepdims=True))
        for k in range(0, per_tile, per_piece):
            totals_ref[i * (per_tile // per_piece) + k // per_piece] = jnp.concatenate(
                found[k : k + per_piece], axis=0
            )
        return 0

    lax.fori_loop(0, width // LANES, step, 0, unroll=8)


def output_kernel(
    sums_ref, mixed_ref, query_ref, scaled_ref, gain_ref, normed_ref, query_grad_ref
):
    taps, width = mixed_ref.shape
    recip, pull = norm_terms(sums_ref, taps)
    for i in range(0, width, LANES):
        lanes = slice(i, i + LANES)
        mixed = mixed_ref[:, lanes]
        lifted = query_ref[:, lanes].astype(F32) * mixed
        normed_ref[:, lanes] = (lifted * recip * gain_ref[:, lanes]).astype(BF16)
        query_grad_ref[:, lanes] = (
            (recip * scaled_ref[:, lanes] - lifted * pull) * mixed
        ).astype(BF16)


def back_kernel(
    filters_ref, conv_ref, after_ref, key_ref, value_ref, key_grad_ref, value_grad_ref
):
    groups, taps = filters_ref.shape
    width = conv_ref.shape[1]
    per_tile = groups * LANES // width
    members = LANES // per_tile
    row, col = index((taps, taps), 0), index((taps, taps), 1)
    own = col >= row
    owner = col // members

    def step(i, _):
        lanes = pl.ds(pl.multiple_of(i * LANES, LANES), LANES)
        window = jnp.concatenate([conv_ref[:, lanes], after_ref[:, lanes]], axis=0)
        acc = None
        for k in range(per_tile):
            own_taps = filters_ref[pl.ds(i * per_tile + k, 1), :].astype(BF16).astype(F32)
            c = rolled(own_taps, taps)
            weights = jnp.concatenate(
                [jnp.where(own, c, 0.0).astype(BF16), jnp.where(own, 0.0, c).astype(BF16)], axis=1
            )
            out = jnp.dot(weights, window, preferred_element_type=F32)
            acc = out if acc is None else jnp.where(owner == k, out, acc)
        key_grad_ref[:, lanes] = (acc * value_ref[:, lanes].astype(F32)).astype(BF16)
        value_grad_ref[:, lanes] = (acc * key_ref[:, lanes].astype(F32)).astype(BF16)
        return 0

    lax.fori_loop(0, width // LANES, step, 0, unroll=8)


def gather_sum_kernel(parts_ref, out_ref):
    out_ref[...] = jnp.broadcast_to(jnp.sum(parts_ref[...], axis=0)[None], out_ref.shape)


def body(query, key_in, value_in, cotangent, filters, norm_gain):
    _, taps, width = query.shape
    groups = filters.shape[0]
    query, key_in, value_in, cotangent = (
        a.reshape(taps, width) for a in (query, key_in, value_in, cotangent)
    )
    gain = norm_gain.reshape(1, width)
    block = shaped((taps, width), BF16)
    peers = lax.axis_size("chan")
    near, far = lax.axis_size("near"), lax.axis_size("far")
    conv_flops = 4 * groups * taps * taps * LANES

    signal = (key_in.astype(F32) * value_in.astype(F32)).astype(BF16)
    before = shifted(signal, CTX, 1)
    wide = shaped((taps, width), F32)
    weights, mirror, held, scaled = call(
        prepare_kernel,
        [shaped((groups, taps, 2 * taps), BF16), block, block, wide],
        filters, signal, query, cotangent, gain,
        scratch=[
            pltpu.VMEM((groups, taps), F32),
            pltpu.VMEM((groups, taps), F32),
            pltpu.VMEM((taps, width), BF16),
            pltpu.VMEM((1, width), F32),
            pltpu.SemaphoreType.DMA((4,)),
        ],
        outside=(0, 2, 3, 4),
    )
    mixed, sums = call(
        mix_kernel,
        [wide, shaped((peers, 2, taps), F32)],
        weights, before, signal, held, scaled,
        flops=conv_flops,
    )
    sums = exchanged(sums, "chan")
    conv, totals = call(
        filter_kernel,
        [block, shaped((near, groups // near, taps), F32)],
        sums, mixed, held, scaled, before, mirror,
        flops=conv_flops,
    )
    totals = exchanged(totals, "near")
    (totals,) = call(gather_sum_kernel, [shaped((far, groups // near, taps), F32)], totals)
    totals = exchanged(totals, "far", far // 2)
    after = shifted(conv, CTX, -1)
    (totals,) = call(gather_sum_kernel, [shaped((near, groups // near, taps), F32)], totals)
    grad_filters = exchanged(totals, "near").reshape(groups, taps)
    normed, grad_query = call(
        output_kernel, [block, block], sums, mixed, held, scaled, gain
    )
    after, normed, grad_query = lax.optimization_barrier((after, normed, grad_query))
    grad_key, grad_value = call(
        back_kernel, [block, block], filters, conv, after, key_in, value_in,
        flops=conv_flops,
    )
    return tuple(a[None] for a in (normed, grad_query, grad_key, grad_value)) + (grad_filters,)


def solution(mesh):
    torus = Mesh(
        mesh.devices.reshape(16, 8, mesh.shape["chan"]), ("far", "near", "chan")
    )
    rows = P(None, CTX, "chan")
    in_specs = (rows, rows, rows, rows, P("chan", None), P("chan"))
    out_specs = (rows, rows, rows, rows, P("chan", None))

    return jax.shard_map(body, mesh=torus, in_specs=in_specs, out_specs=out_specs, check_vma=False)
```

```python
import math

import jax
import jax.numpy as jnp
from jax import lax
from jax.experimental import pallas as pl
from jax.experimental.pallas import tpu as pltpu
from jax.sharding import Mesh
from jax.sharding import PartitionSpec as P


D = 8192
CTX = ("far", "near")
LANES = 128
VMEM_LIMIT = 16 * 2**20
F32 = jnp.float32
BF16 = jnp.bfloat16


def shifted(block, axes, distance):
    devices = range(lax.axis_size(axes))
    route = [(i - distance, i) for i in devices if i - distance in devices]
    return lax.ppermute(block, axes, route)


def exchanged(x, axis, first=0):
    size = lax.axis_size(axis)
    order = [[(i + first) % size for i in range(size)]] if first else None
    return lax.all_to_all(x, axis, 0, 0, axis_index_groups=order, tiled=True)


def call(kernel, outs, *args, flops=0, scratch=(), outside=()):
    moved = sum(a.size * a.dtype.itemsize for a in args)
    moved += sum(math.prod(o.shape) * o.dtype.itemsize for o in outs)
    vmem = pl.BlockSpec(memory_space=pltpu.VMEM)
    hbm = pl.BlockSpec(memory_space=pltpu.HBM)
    args = [
        pltpu.with_memory_space_constraint(a, pltpu.HBM) if i in outside else a
        for i, a in enumerate(args)
    ]
    return pl.pallas_call(
        kernel,
        out_shape=outs,
        in_specs=[hbm if i in outside else vmem for i in range(len(args))],
        out_specs=[vmem] * len(outs),
        scratch_shapes=scratch,
        compiler_params=pltpu.CompilerParams(vmem_limit_bytes=VMEM_LIMIT),
        cost_estimate=pl.CostEstimate(flops=flops, bytes_accessed=moved, transcendentals=0),
    )(*args)


def shaped(shape, dtype):
    return jax.ShapeDtypeStruct(shape, dtype)


def rolled(row, taps, shift=0):
    full = jnp.broadcast_to(row, (taps, row.shape[1]))
    return pltpu.roll(full, shift, 1, stride=1, stride_axis=0)


def index(shape, dim):
    return lax.broadcasted_iota(jnp.int32, shape, dim)


def column(row, taps):
    return jnp.broadcast_to(row, (taps, taps)).T


def prepare_kernel(
    filters_ref, signal_ref, query_ref, cot_ref, gain_ref,
    weights_ref, mirror_ref, held_ref, scaled_ref, taps_ref, back_taps_ref, cot_copy, gain_copy, sems,
):
    groups, taps = filters_ref.shape
    copies = [
        pltpu.make_async_copy(source, target, sems.at[i])
        for i, (source, target) in enumerate(
            [(filters_ref, taps_ref), (gain_ref, gain_copy), (cot_ref, cot_copy), (query_ref, held_ref)]
        )
    ]
    for copy in copies:
        copy.start()
    row, col = index((taps, taps), 0), index((taps, taps), 1)
    swap = (row + col == taps - 1).astype(BF16)
    mirror_ref[...] = jnp.dot(swap, signal_ref[...], preferred_element_type=F32).astype(BF16)
    copies[0].wait()
    own = row >= col
    turn = (lax.rem(row + col, taps) == 0).astype(BF16)
    back_taps_ref[...] = jnp.dot(
        taps_ref[...].astype(BF16), turn, preferred_element_type=F32
    )

    def step(g, _):
        c = rolled(back_taps_ref[pl.ds(g, 1), :], taps)
        weights_ref[g, :, :taps] = jnp.where(own, 0.0, c).astype(BF16)
        weights_ref[g, :, taps:] = jnp.where(own, c, 0.0).astype(BF16)
        return 0

    lax.fori_loop(0, groups, step, 0, unroll=8)
    for copy in copies[1:]:
        copy.wait()
    scaled_ref[...] = gain_copy[...] * cot_copy[...].astype(F32)


def mix_kernel(weights_ref, before_ref, signal_ref, query_ref, scaled_ref, mixed_ref, sums_ref):
    groups, taps, _ = weights_ref.shape
    width = signal_ref.shape[1]
    per_tile = groups * LANES // width
    members = LANES // per_tile
    owner = index((taps, LANES), 1) // members

    def step(i, totals):
        lanes = pl.ds(pl.multiple_of(i * LANES, LANES), LANES)
        window = jnp.concatenate([before_ref[:, lanes], signal_ref[:, lanes]], axis=0)
        acc = None
        for k in range(per_tile):
            out = jnp.dot(weights_ref[i * per_tile + k], window, preferred_element_type=F32)
            acc = out if acc is None else jnp.where(owner == k, out, acc)
        mixed_ref[:, lanes] = acc
        lifted = query_ref[:, lanes].astype(F32) * acc
        return totals[0] + lifted * lifted, totals[1] + scaled_ref[:, lanes] * lifted

    zero = jnp.zeros((taps, LANES), F32)
    power, inner = lax.fori_loop(0, width // LANES, step, (zero, zero), unroll=8)
    sums = jnp.concatenate(
        [jnp.sum(power.T, axis=0, keepdims=True), jnp.sum(inner.T, axis=0, keepdims=True)], axis=0
    )
    sums_ref[...] = jnp.broadcast_to(sums[None], sums_ref.shape)


def norm_terms(sums_ref, taps):
    sums = jnp.sum(sums_ref[...], axis=0)
    recip = lax.rsqrt(sums[0:1] / D + 1e-6)
    pull = recip * recip * recip * sums[1:2] / D
    return column(recip, taps), column(pull, taps)


def filter_kernel(
    sums_ref, mixed_ref, query_ref, scaled_ref, before_ref, mirror_ref, conv_ref, totals_ref
):
    taps, width = conv_ref.shape
    pieces, per_piece, _ = totals_ref.shape
    groups = pieces * per_piece
    per_tile = groups * LANES // width
    members = LANES // per_tile
    row, col = index((taps, taps), 0), index((taps, taps), 1)
    own = row + col >= taps - 1
    swap = (row + col == taps - 1).astype(BF16)
    owner = col // members
    recip, pull = norm_terms(sums_ref, taps)

    def step(i, _):
        lanes = pl.ds(pl.multiple_of(i * LANES, LANES), LANES)
        query = query_ref[:, lanes].astype(F32)
        grad_mix = recip * scaled_ref[:, lanes] - query * mixed_ref[:, lanes] * pull
        conv = (grad_mix * query).astype(BF16)
        conv_ref[:, lanes] = conv
        past = jnp.dot(swap, before_ref[:, lanes], preferred_element_type=F32).astype(BF16)
        window = jnp.concatenate([past, mirror_ref[:, lanes]], axis=0)
        found = []
        for k in range(per_tile):
            mine = jnp.where(owner == k, conv, jnp.zeros_like(conv))
            pairs = lax.dot_general(
                mine, window, (((1,), (1,)), ((), ())), preferred_element_type=F32
            )
            both = jnp.where(own, pairs[:, taps:], pairs[:, :taps])
            lined = pltpu.roll(both, 1, 1, stride=1, stride_axis=0)
            found.append(jnp.sum(lined, axis=0, keepdims=True))
        for k in range(0, per_tile, per_piece):
            totals_ref[i * (per_tile // per_piece) + k // per_piece] = jnp.concatenate(
                found[k : k + per_piece], axis=0
            )
        return 0

    lax.fori_loop(0, width // LANES, step, 0, unroll=8)


def output_kernel(
    sums_ref, mixed_ref, query_ref, scaled_ref, gain_ref, normed_ref, query_grad_ref
):
    taps, width = mixed_ref.shape
    recip, pull = norm_terms(sums_ref, taps)
    for i in range(0, width, LANES):
        lanes = slice(i, i + LANES)
        mixed = mixed_ref[:, lanes]
        lifted = query_ref[:, lanes].astype(F32) * mixed
        normed_ref[:, lanes] = (lifted * recip * gain_ref[:, lanes]).astype(BF16)
        query_grad_ref[:, lanes] = (
            (recip * scaled_ref[:, lanes] - lifted * pull) * mixed
        ).astype(BF16)


def back_kernel(
    filters_ref, conv_ref, after_ref, key_ref, value_ref, key_grad_ref, value_grad_ref
):
    groups, taps = filters_ref.shape
    width = conv_ref.shape[1]
    per_tile = groups * LANES // width
    members = LANES // per_tile
    row, col = index((taps, taps), 0), index((taps, taps), 1)
    own = col >= row
    owner = col // members

    def step(i, _):
        lanes = pl.ds(pl.multiple_of(i * LANES, LANES), LANES)
        window = jnp.concatenate([conv_ref[:, lanes], after_ref[:, lanes]], axis=0)
        acc = None
        for k in range(per_tile):
            own_taps = filters_ref[pl.ds(i * per_tile + k, 1), :].astype(BF16).astype(F32)
            c = rolled(own_taps, taps)
            weights = jnp.concatenate(
                [jnp.where(own, c, 0.0).astype(BF16), jnp.where(own, 0.0, c).astype(BF16)], axis=1
            )
            out = jnp.dot(weights, window, preferred_element_type=F32)
            acc = out if acc is None else jnp.where(owner == k, out, acc)
        key_grad_ref[:, lanes] = (acc * value_ref[:, lanes].astype(F32)).astype(BF16)
        value_grad_ref[:, lanes] = (acc * key_ref[:, lanes].astype(F32)).astype(BF16)
        return 0

    lax.fori_loop(0, width // LANES, step, 0, unroll=8)


def gather_sum_kernel(parts_ref, out_ref):
    total = jnp.sum(parts_ref[...].astype(F32), axis=0).astype(out_ref.dtype)
    out_ref[...] = jnp.broadcast_to(total[None], out_ref.shape)


def body(query, key_in, value_in, cotangent, filters, norm_gain):
    _, taps, width = query.shape
    groups = filters.shape[0]
    query, key_in, value_in, cotangent = (
        a.reshape(taps, width) for a in (query, key_in, value_in, cotangent)
    )
    gain = norm_gain.reshape(1, width)
    block = shaped((taps, width), BF16)
    peers = lax.axis_size("chan")
    near, far = lax.axis_size("near"), lax.axis_size("far")
    conv_flops = 4 * groups * taps * taps * LANES

    signal = (key_in.astype(F32) * value_in.astype(F32)).astype(BF16)
    before = shifted(signal, CTX, 1)
    wide = shaped((taps, width), F32)
    weights, mirror, held, scaled = call(
        prepare_kernel,
        [shaped((groups, taps, 2 * taps), BF16), block, block, wide],
        filters, signal, query, cotangent, gain,
        scratch=[
            pltpu.VMEM((groups, taps), F32),
            pltpu.VMEM((groups, taps), F32),
            pltpu.VMEM((taps, width), BF16),
            pltpu.VMEM((1, width), F32),
            pltpu.SemaphoreType.DMA((4,)),
        ],
        outside=(0, 2, 3, 4),
    )
    mixed, sums = call(
        mix_kernel,
        [wide, shaped((peers, 2, taps), F32)],
        weights, before, signal, held, scaled,
        flops=conv_flops,
    )
    sums = exchanged(sums, "chan")
    conv, totals = call(
        filter_kernel,
        [block, shaped((near, groups // near, taps), F32)],
        sums, mixed, held, scaled, before, mirror,
        flops=conv_flops,
    )
    totals = exchanged(totals, "near")
    (totals,) = call(gather_sum_kernel, [shaped((far, groups // near, taps), BF16)], totals)
    totals = exchanged(totals, "far", far // 2)
    after = shifted(conv, CTX, -1)
    (totals,) = call(gather_sum_kernel, [shaped((near, groups // near, taps), F32)], totals)
    grad_filters = exchanged(totals, "near").reshape(groups, taps)
    normed, grad_query = call(
        output_kernel, [block, block], sums, mixed, held, scaled, gain
    )
    after, normed, grad_query = lax.optimization_barrier((after, normed, grad_query))
    grad_key, grad_value = call(
        back_kernel, [block, block], filters, conv, after, key_in, value_in,
        flops=conv_flops,
    )
    return tuple(a[None] for a in (normed, grad_query, grad_key, grad_value)) + (grad_filters,)


def solution(mesh):
    torus = Mesh(
        mesh.devices.reshape(16, 8, mesh.shape["chan"]), ("far", "near", "chan")
    )
    rows = P(None, CTX, "chan")
    in_specs = (rows, rows, rows, rows, P("chan", None), P("chan"))
    out_specs = (rows, rows, rows, rows, P("chan", None))

    return jax.shard_map(body, mesh=torus, in_specs=in_specs, out_specs=out_specs, check_vma=False)
```

```python
import math

import jax
import jax.numpy as jnp
from jax import lax
from jax.experimental import pallas as pl
from jax.experimental.pallas import tpu as pltpu
from jax.sharding import Mesh
from jax.sharding import PartitionSpec as P


D = 8192
CTX = ("far", "near")
LANES = 128
VMEM_LIMIT = 16 * 2**20
F32 = jnp.float32
BF16 = jnp.bfloat16


def shifted(block, axes, distance):
    devices = range(lax.axis_size(axes))
    route = [(i - distance, i) for i in devices if i - distance in devices]
    return lax.ppermute(block, axes, route)


def exchanged(x, axis, first=0):
    size = lax.axis_size(axis)
    order = [[(i + first) % size for i in range(size)]] if first else None
    return lax.all_to_all(x, axis, 0, 0, axis_index_groups=order, tiled=True)


def call(kernel, outs, *args, flops=0, scratch=(), outside=()):
    moved = sum(a.size * a.dtype.itemsize for a in args)
    moved += sum(math.prod(o.shape) * o.dtype.itemsize for o in outs)
    vmem = pl.BlockSpec(memory_space=pltpu.VMEM)
    hbm = pl.BlockSpec(memory_space=pltpu.HBM)
    args = [
        pltpu.with_memory_space_constraint(a, pltpu.HBM) if i in outside else a
        for i, a in enumerate(args)
    ]
    return pl.pallas_call(
        kernel,
        out_shape=outs,
        in_specs=[hbm if i in outside else vmem for i in range(len(args))],
        out_specs=[vmem] * len(outs),
        scratch_shapes=scratch,
        compiler_params=pltpu.CompilerParams(vmem_limit_bytes=VMEM_LIMIT),
        cost_estimate=pl.CostEstimate(flops=flops, bytes_accessed=moved, transcendentals=0),
    )(*args)


def shaped(shape, dtype):
    return jax.ShapeDtypeStruct(shape, dtype)


def rolled(row, taps, shift=0):
    full = jnp.broadcast_to(row, (taps, row.shape[1]))
    return pltpu.roll(full, shift, 1, stride=1, stride_axis=0)


def index(shape, dim):
    return lax.broadcasted_iota(jnp.int32, shape, dim)


def column(row, taps):
    return jnp.broadcast_to(row, (taps, taps)).T


def prepare_kernel(
    filters_ref, signal_ref, query_ref, cot_ref, gain_ref,
    weights_ref, near_ref, mirror_ref, held_ref, scaled_ref, own_ref, taps_ref, back_taps_ref, cot_copy, gain_copy, sems,
):
    groups, taps = filters_ref.shape
    copies = [
        pltpu.make_async_copy(source, target, sems.at[i])
        for i, (source, target) in enumerate(
            [(filters_ref, taps_ref), (gain_ref, gain_copy), (cot_ref, cot_copy), (query_ref, held_ref)]
        )
    ]
    for copy in copies:
        copy.start()
    row, col = index((taps, taps), 0), index((taps, taps), 1)
    swap = (row + col == taps - 1).astype(BF16)
    mirror_ref[...] = jnp.dot(swap, signal_ref[...], preferred_element_type=F32).astype(BF16)
    copies[0].wait()
    own = row >= col
    turn = (lax.rem(row + col, taps) == 0).astype(BF16)
    back_taps_ref[...] = jnp.dot(
        taps_ref[...].astype(BF16), turn, preferred_element_type=F32
    )

    def step(g, _):
        c = rolled(back_taps_ref[pl.ds(g, 1), :], taps)
        weights_ref[g] = jnp.where(own, 0.0, c).astype(BF16)
        own_ref[g] = jnp.where(own, c, 0.0).astype(BF16)
        return 0

    lax.fori_loop(0, groups, step, 0, unroll=8)
    width = signal_ref.shape[1]
    per_tile = groups * LANES // width
    owner = index((taps, LANES), 1) // (LANES // per_tile)

    def tile(i, _):
        lanes = pl.ds(pl.multiple_of(i * LANES, LANES), LANES)
        acc = None
        for k in range(per_tile):
            out = jnp.dot(
                own_ref[i * per_tile + k], signal_ref[:, lanes], preferred_element_type=F32
            )
            acc = out if acc is None else jnp.where(owner == k, out, acc)
        near_ref[:, lanes] = acc
        return 0

    lax.fori_loop(0, width // LANES, tile, 0, unroll=2)
    for copy in copies[1:]:
        copy.wait()
    scaled_ref[...] = gain_copy[...] * cot_copy[...].astype(F32)


def mix_kernel(weights_ref, before_ref, near_ref, query_ref, scaled_ref, mixed_ref, sums_ref):
    groups, taps, _ = weights_ref.shape
    width = before_ref.shape[1]
    per_tile = groups * LANES // width
    members = LANES // per_tile
    owner = index((taps, LANES), 1) // members

    def step(i, totals):
        lanes = pl.ds(pl.multiple_of(i * LANES, LANES), LANES)
        window = before_ref[:, lanes]
        acc = None
        for k in range(per_tile):
            out = jnp.dot(weights_ref[i * per_tile + k], window, preferred_element_type=F32)
            acc = out if acc is None else jnp.where(owner == k, out, acc)
        acc = acc + near_ref[:, lanes]
        mixed_ref[:, lanes] = acc
        lifted = query_ref[:, lanes].astype(F32) * acc
        return totals[0] + lifted * lifted, totals[1] + scaled_ref[:, lanes] * lifted

    zero = jnp.zeros((taps, LANES), F32)
    power, inner = lax.fori_loop(0, width // LANES, step, (zero, zero), unroll=8)
    sums = jnp.concatenate(
        [jnp.sum(power.T, axis=0, keepdims=True), jnp.sum(inner.T, axis=0, keepdims=True)], axis=0
    )
    sums_ref[...] = jnp.broadcast_to(sums[None], sums_ref.shape)


def norm_terms(sums_ref, taps):
    sums = jnp.sum(sums_ref[...], axis=0)
    recip = lax.rsqrt(sums[0:1] / D + 1e-6)
    pull = recip * recip * recip * sums[1:2] / D
    return column(recip, taps), column(pull, taps)


def filter_kernel(
    sums_ref, mixed_ref, query_ref, scaled_ref, before_ref, mirror_ref, conv_ref, totals_ref
):
    taps, width = conv_ref.shape
    pieces, per_piece, _ = totals_ref.shape
    groups = pieces * per_piece
    per_tile = groups * LANES // width
    members = LANES // per_tile
    row, col = index((taps, taps), 0), index((taps, taps), 1)
    own = row + col >= taps - 1
    swap = (row + col == taps - 1).astype(BF16)
    owner = col // members
    recip, pull = norm_terms(sums_ref, taps)

    def step(i, _):
        lanes = pl.ds(pl.multiple_of(i * LANES, LANES), LANES)
        query = query_ref[:, lanes].astype(F32)
        grad_mix = recip * scaled_ref[:, lanes] - query * mixed_ref[:, lanes] * pull
        conv = (grad_mix * query).astype(BF16)
        conv_ref[:, lanes] = conv
        past = jnp.dot(swap, before_ref[:, lanes], preferred_element_type=F32).astype(BF16)
        window = jnp.concatenate([past, mirror_ref[:, lanes]], axis=0)
        found = []
        for k in range(per_tile):
            mine = jnp.where(owner == k, conv, jnp.zeros_like(conv))
            pairs = lax.dot_general(
                mine, window, (((1,), (1,)), ((), ())), preferred_element_type=F32
            )
            both = jnp.where(own, pairs[:, taps:], pairs[:, :taps])
            lined = pltpu.roll(both, 1, 1, stride=1, stride_axis=0)
            found.append(jnp.sum(lined, axis=0, keepdims=True))
        for k in range(0, per_tile, per_piece):
            totals_ref[i * (per_tile // per_piece) + k // per_piece] = jnp.concatenate(
                found[k : k + per_piece], axis=0
            )
        return 0

    lax.fori_loop(0, width // LANES, step, 0, unroll=8)


def output_kernel(
    sums_ref, mixed_ref, query_ref, scaled_ref, gain_ref, normed_ref, query_grad_ref
):
    taps, width = mixed_ref.shape
    recip, pull = norm_terms(sums_ref, taps)
    for i in range(0, width, LANES):
        lanes = slice(i, i + LANES)
        mixed = mixed_ref[:, lanes]
        lifted = query_ref[:, lanes].astype(F32) * mixed
        normed_ref[:, lanes] = (lifted * recip * gain_ref[:, lanes]).astype(BF16)
        query_grad_ref[:, lanes] = (
            (recip * scaled_ref[:, lanes] - lifted * pull) * mixed
        ).astype(BF16)


def back_kernel(
    filters_ref, conv_ref, after_ref, key_ref, value_ref, key_grad_ref, value_grad_ref
):
    groups, taps = filters_ref.shape
    width = conv_ref.shape[1]
    per_tile = groups * LANES // width
    members = LANES // per_tile
    row, col = index((taps, taps), 0), index((taps, taps), 1)
    own = col >= row
    owner = col // members

    def step(i, _):
        lanes = pl.ds(pl.multiple_of(i * LANES, LANES), LANES)
        window = jnp.concatenate([conv_ref[:, lanes], after_ref[:, lanes]], axis=0)
        acc = None
        for k in range(per_tile):
            own_taps = filters_ref[pl.ds(i * per_tile + k, 1), :].astype(BF16).astype(F32)
            c = rolled(own_taps, taps)
            weights = jnp.concatenate(
                [jnp.where(own, c, 0.0).astype(BF16), jnp.where(own, 0.0, c).astype(BF16)], axis=1
            )
            out = jnp.dot(weights, window, preferred_element_type=F32)
            acc = out if acc is None else jnp.where(owner == k, out, acc)
        key_grad_ref[:, lanes] = (acc * value_ref[:, lanes].astype(F32)).astype(BF16)
        value_grad_ref[:, lanes] = (acc * key_ref[:, lanes].astype(F32)).astype(BF16)
        return 0

    lax.fori_loop(0, width // LANES, step, 0, unroll=8)


def gather_sum_kernel(parts_ref, out_ref):
    total = jnp.sum(parts_ref[...].astype(F32), axis=0).astype(out_ref.dtype)
    out_ref[...] = jnp.broadcast_to(total[None], out_ref.shape)


def body(query, key_in, value_in, cotangent, filters, norm_gain):
    _, taps, width = query.shape
    groups = filters.shape[0]
    query, key_in, value_in, cotangent = (
        a.reshape(taps, width) for a in (query, key_in, value_in, cotangent)
    )
    gain = norm_gain.reshape(1, width)
    block = shaped((taps, width), BF16)
    peers = lax.axis_size("chan")
    near, far = lax.axis_size("near"), lax.axis_size("far")
    conv_flops = 4 * groups * taps * taps * LANES

    signal = (key_in.astype(F32) * value_in.astype(F32)).astype(BF16)
    before = shifted(signal, CTX, 1)
    wide = shaped((taps, width), F32)
    weights, near_mixed, mirror, held, scaled = call(
        prepare_kernel,
        [shaped((groups, taps, taps), BF16), wide, block, block, wide],
        filters, signal, query, cotangent, gain,
        scratch=[
            pltpu.VMEM((groups, taps, taps), BF16),
            pltpu.VMEM((groups, taps), F32),
            pltpu.VMEM((groups, taps), F32),
            pltpu.VMEM((taps, width), BF16),
            pltpu.VMEM((1, width), F32),
            pltpu.SemaphoreType.DMA((4,)),
        ],
        outside=(0, 2, 3, 4),
    )
    mixed, sums = call(
        mix_kernel,
        [wide, shaped((peers, 2, taps), F32)],
        weights, before, near_mixed, held, scaled,
        flops=conv_flops,
    )
    sums = exchanged(sums, "chan")
    conv, totals = call(
        filter_kernel,
        [block, shaped((near, groups // near, taps), F32)],
        sums, mixed, held, scaled, before, mirror,
        flops=conv_flops,
    )
    totals = exchanged(totals, "near")
    (totals,) = call(gather_sum_kernel, [shaped((far, groups // near, taps), BF16)], totals)
    totals = exchanged(totals, "far", far // 2)
    after = shifted(conv, CTX, -1)
    (totals,) = call(gather_sum_kernel, [shaped((near, groups // near, taps), F32)], totals)
    grad_filters = exchanged(totals, "near").reshape(groups, taps)
    normed, grad_query = call(
        output_kernel, [block, block], sums, mixed, held, scaled, gain
    )
    after, normed, grad_query = lax.optimization_barrier((after, normed, grad_query))
    grad_key, grad_value = call(
        back_kernel, [block, block], filters, conv, after, key_in, value_in,
        flops=conv_flops,
    )
    return tuple(a[None] for a in (normed, grad_query, grad_key, grad_value)) + (grad_filters,)


def solution(mesh):
    torus = Mesh(
        mesh.devices.reshape(16, 8, mesh.shape["chan"]), ("far", "near", "chan")
    )
    rows = P(None, CTX, "chan")
    in_specs = (rows, rows, rows, rows, P("chan", None), P("chan"))
    out_specs = (rows, rows, rows, rows, P("chan", None))

    return jax.shard_map(body, mesh=torus, in_specs=in_specs, out_specs=out_specs, check_vma=False)
```
